256 devices in a mesh: rows: 8 (over z), feat: 4 (over y_lo, core), cls: 8 (over y_hi, x).
Axes of the slice: x: 4, y: 4 (y_hi: 2, y_lo: 2; y = y_hi * 2 + y_lo), z: 8, core: 2. Of those that a mesh axis runs over, the one named last changes fastest.
Arguments:
- bins: int32 [16384, 256], P('rows', 'feat'), may hold values from 0 to 255
- logits: float32 [16384, 32], P('rows', 'cls'), may hold values from -16 to 400
- labels: int32 [16384], P('rows'), may hold values from 0 to 31
- node_ids: int32 [16384], P('rows'), may hold values from 0 to 31
- small_flag: int32 [16], replicated, may hold values from 0 to 1
- parent_grad: float32 [16, 256, 32, 256], P(None, ('feat', 'rows'), 'cls'), may hold values from -3 to 3
- parent_hess: float32 [16, 256, 32, 256], P(None, ('feat', 'rows'), 'cls'), may hold values from 0.01 to 1
Outputs:
- child_grad: float32 [32, 256, 32, 256], P(None, ('feat', 'rows'), 'cls')
- child_hess: float32 [32, 256, 32, 256], P(None, ('feat', 'rows'), 'cls')
- gains: float32 [32, 256, 256], P(None, ('feat', 'rows'))
- best_gain: float32 [32], replicated
The draws below stay inside these ranges and needn't reach their ends.
All inputs are finite; a program needn't handle non-finite values.
Results may differ from the reference program's by a relative error of at most 0.00047.
Values may be sent and summed in bfloat16 or wider, within the bound.
A program may use at most 64 MiB of HBM per device.

```python
import math
import jax
import jax.numpy as jnp
import numpy as np
from jax import lax

C = 32
F = 256
B = 256
P_SIZE = 16
ROWS = 16384
NODES = 32


def draw_logits(key, part):
    key_first = jax.random.fold_in(key, 0)
    return jnp.clip(3.0 * jax.random.normal(key_first, (ROWS, C), jnp.float32), -15.0, 15.0)


def place_ends(drawn, own_key, low, top_value):
    spot = [jax.random.randint(jax.random.fold_in(own_key, axis), (), 0, length) for axis, length in enumerate(drawn.shape)]
    widest = drawn.shape.index(max(drawn.shape))
    beside = spot[:widest] + [(spot[widest] + 1) % drawn.shape[widest]] + spot[widest + 1:]
    return drawn.at[tuple(spot)].set(low).at[tuple(beside)].set(top_value)


def level_of(own_key, extent, shards, smallest, top_value):
    gain = 1.0
    for position, parts in shards:
        heights = jax.random.uniform(jax.random.fold_in(jax.random.fold_in(own_key, 6), position), (parts,), jnp.float32, smallest / len(shards), top_value / len(shards))
        gain = gain * jnp.repeat(jnp.exp(heights), extent[position] // parts).reshape((-1,) + (1,) * (len(extent) - 1 - position))
    return gain


def rank_table(number_of, skew):
    portions = [(1 << 20) // math.isqrt(grade ** skew) + 1 for grade in range(1, number_of + 1)]
    scale = 1 + sum(portions) // (1 << 30)
    return np.cumsum(np.array([max(1, weight // scale) for weight in portions]))


def ranked_ids(own_key, dims, number_of, slope):
    table = rank_table(number_of, slope)
    pick = jax.random.randint(jax.random.fold_in(own_key, 1), dims, 0, int(table[number_of - 1]))
    rank = jnp.searchsorted(jnp.asarray(table, jnp.int32), pick, side="right")
    return jax.random.permutation(jax.random.fold_in(own_key, 2), number_of)[rank].astype(jnp.int32)


def bell_draw(stream_key, shape, deviation, reach, cuts=(), held_as=jnp.bfloat16):
    values = deviation * jax.random.normal(stream_key, shape, jnp.float32)
    if cuts:
        values = values * level_of(stream_key, shape, cuts, -0.22, 0.18)
    return jnp.clip(values, -reach, reach).astype(held_as)


def setup_inputs(seed: int = 0) -> dict:
    seeds = jax.random.split(jax.random.key(seed), 8)
    return {
        "bins": place_ends(jax.random.randint(seeds[0], (ROWS, F), 0, B), jax.random.fold_in(seeds[0], 1), 0, B - 1).astype(jnp.int32),
        "logits": draw_logits(jax.random.fold_in(seeds[7], 71), 0),
        "labels": place_ends(jax.random.randint(seeds[2], (ROWS,), 0, C), jax.random.fold_in(seeds[2], 1), 0, C - 1).astype(jnp.int32),
        "node_ids": place_ends(ranked_ids(seeds[3], (ROWS,), NODES, 2), jax.random.fold_in(seeds[3], 3), 0, NODES - 1).astype(jnp.int32),
        "small_flag": place_ends(jax.random.randint(seeds[4], (P_SIZE,), 0, 2), jax.random.fold_in(seeds[4], 1), 0, 1).astype(jnp.int32),
        "parent_grad": bell_draw(seeds[5], (P_SIZE, F, C, B), 0.5, 3.0, ((1, 32), (2, 8)), jnp.float32),
        "parent_hess": jnp.clip(jnp.exp(math.log(1.0) - 4.6051702 * jax.random.uniform(seeds[6], (P_SIZE, F, C, B), jnp.float32) ** level_of(seeds[6], (P_SIZE, F, C, B), ((1, 32), (2, 8)), -0.2, 0.2)), 0.01, 1.0),
    }


ridge_weight = 1.0


def leaf_term(grad_sum, hess_sum):
    return grad_sum * grad_sum / (jnp.maximum(hess_sum, 0.0) + ridge_weight)


def assemble(small_part, parent_part, small_flag):
    sibling = parent_part - small_part
    flag_zero = (small_flag == 0)[:, None, None, None]
    even_child = jnp.where(flag_zero, small_part, sibling)
    odd_child = jnp.where(flag_zero, sibling, small_part)
    return jnp.stack([even_child, odd_child], axis=1).reshape((-1,) + small_part.shape[1:])


def reference(bins, logits, labels, node_ids, small_flag, parent_grad, parent_hess):
    peak = jnp.max(logits, axis=1, keepdims=True)
    expo = jnp.exp(logits - peak)
    likely = expo / jnp.sum(expo, axis=1, keepdims=True)
    classes = jnp.arange(C, dtype=jnp.int32)
    target = (labels[:, None] == classes[None, :]).astype(jnp.float32)
    gradient = (likely - target).astype(jnp.bfloat16)
    curvature = (likely * (1.0 - likely)).astype(jnp.bfloat16)
    parents = jnp.arange(P_SIZE, dtype=jnp.int32)
    in_small = ((node_ids // 2)[:, None] == parents[None, :]) & ((node_ids % 2)[:, None] == small_flag[None, :])
    stacked = jnp.stack([gradient, curvature], axis=1).astype(jnp.float32)
    columns = (in_small.astype(jnp.float32)[:, :, None, None] * stacked[:, None, :, :]).reshape(ROWS, P_SIZE * 2 * C)

    def per_feature(feature_bins):
        return jax.ops.segment_sum(columns, feature_bins, num_segments=B)

    counted = lax.map(per_feature, bins.T)
    counted = counted.reshape(F, B, P_SIZE, 2, C).transpose(2, 3, 0, 4, 1)
    child_grad = assemble(counted[:, 0], parent_grad, small_flag)
    child_hess = assemble(counted[:, 1], parent_hess, small_flag)
    left_grad = jnp.cumsum(child_grad, axis=-1)
    left_hess = jnp.cumsum(child_hess, axis=-1)
    whole_grad = left_grad[..., -1:]
    whole_hess = left_hess[..., -1:]
    scores = leaf_term(left_grad, left_hess) + leaf_term(whole_grad - left_grad, whole_hess - left_hess) - leaf_term(whole_grad, whole_hess)
    gains = jnp.sum(scores, axis=2) / C
    best_gain = jnp.max(gains, axis=(1, 2))
    return child_grad, child_hess, gains, best_gain
```

```python
import functools

import jax
import jax.numpy as jnp
from jax import lax
from jax.experimental import pallas as pl
from jax.experimental.pallas import tpu as pltpu
from jax.sharding import PartitionSpec as P

ridge_weight = 1.0
NT = (((1,), (1,)), ((), ()))
NN = (((1,), (0,)), ((), ()))


def exchange_kernel(
    bins_ref, logits_ref, labels_ref, node_ref, flag_ref,
    allbins_ref, allslot_ref, allg_ref,
    sendb, stats, b_send, b_recv, s_send, s_recv, t_send, t_recv, g_send, g_recv,
):
    n_row = lax.axis_size("rows")
    n_cls = lax.axis_size("cls")
    me_r = lax.axis_index("rows")
    me_c = lax.axis_index("cls")
    pcount = flag_ref.shape[0]
    c_dev = logits_ref.shape[1]
    rows_here = bins_ref.shape[0]
    f_own = bins_ref.shape[1] // n_row

    barrier = pltpu.get_barrier_semaphore()
    for k in range(1, n_row):
        pl.semaphore_signal(barrier, inc=1, device_id={"rows": lax.rem(me_r + k, n_row)})
    for k in range(1, n_cls):
        pl.semaphore_signal(barrier, inc=1, device_id={"cls": lax.rem(me_c + k, n_cls)})

    bt = jnp.transpose(bins_ref[...].astype(jnp.float32)).astype(jnp.bfloat16)
    sendb[...] = bt.reshape(n_row, f_own, rows_here)
    allbins_ref[me_r] = sendb[me_r]
    node = node_ref[...]
    slot = jnp.full(node.shape, -1.0, jnp.float32)
    for q in range(pcount):
        slot = jnp.where(node == 2 * q + flag_ref[q], float(q), slot)
    allslot_ref[me_r] = slot

    pl.semaphore_wait(barrier, n_row + n_cls - 2)

    copies = []
    for k in range(1, n_row):
        peer = lax.rem(me_r + k, n_row)
        copies.append(pltpu.make_async_remote_copy(
            src_ref=sendb.at[peer], dst_ref=allbins_ref.at[me_r],
            send_sem=b_send.at[k], recv_sem=b_recv.at[k], device_id={"rows": peer}))
        copies[-1].start()
        copies.append(pltpu.make_async_remote_copy(
            src_ref=allslot_ref.at[me_r], dst_ref=allslot_ref.at[me_r],
            send_sem=s_send.at[k], recv_sem=s_recv.at[k], device_id={"rows": peer}))
        copies[-1].start()

    lt = jnp.transpose(logits_ref[...])
    top = jnp.max(lt, axis=0, keepdims=True)
    part = jnp.sum(jnp.exp(lt - top), axis=0, keepdims=True)
    stats[me_c] = jnp.concatenate([top, part], axis=0)
    stat_copies = []
    for k in range(1, n_cls):
        peer = lax.rem(me_c + k, n_cls)
        stat_copies.append(pltpu.make_async_remote_copy(
            src_ref=stats.at[me_c], dst_ref=stats.at[me_c],
            send_sem=t_send.at[k], recv_sem=t_recv.at[k], device_id={"cls": peer}))
        stat_copies[-1].start()
    for c in stat_copies:
        c.wait_recv()
    tops = [stats[d, 0:1, :] for d in range(n_cls)]
    peak = functools.reduce(jnp.maximum, tops)
    denom = functools.reduce(
        jnp.add, [stats[d, 1:2, :] * jnp.exp(tops[d] - peak) for d in range(n_cls)])
    likely = jnp.exp(lt - peak) / denom
    classes = me_c * c_dev + lax.broadcasted_iota(jnp.int32, lt.shape, 0)
    target = (labels_ref[...] == classes).astype(jnp.float32)
    both = jnp.concatenate([likely - target, likely * (1.0 - likely)], axis=0)
    allg_ref[me_r] = both.astype(jnp.bfloat16)
    for k in range(1, n_row):
        peer = lax.rem(me_r + k, n_row)
        copies.append(pltpu.make_async_remote_copy(
            src_ref=allg_ref.at[me_r], dst_ref=allg_ref.at[me_r],
            send_sem=g_send.at[k], recv_sem=g_recv.at[k], device_id={"rows": peer}))
        copies[-1].start()
    for c in stat_copies:
        c.wait_send()
    for c in copies:
        c.wait()


def leaf_term(grad_sum, hess_sum):
    return grad_sum * grad_sum / (jnp.maximum(hess_sum, 0.0) + ridge_weight)


def split3(x):
    hi = x.astype(jnp.bfloat16)
    rest = x - hi.astype(jnp.float32)
    mid = rest.astype(jnp.bfloat16)
    low = (rest - mid.astype(jnp.float32)).astype(jnp.bfloat16)
    return hi, mid, low


def level_kernel(
    bins_ref, slot_ref, g_ref, flag_ref, pg_ref, ph_ref,
    cg_ref, ch_ref, gain_ref, acc,
):
    n_src, f_own, rows_src = bins_ref.shape
    kc = g_ref.shape[1]
    c_dev = kc // 2
    pcount = flag_ref.shape[0]
    levels = pg_ref.shape[3]
    chunk = 1024
    per_src = rows_src // chunk
    iota = lax.broadcasted_iota(jnp.int32, (levels, chunk), 0).astype(jnp.bfloat16)
    acc[...] = jnp.zeros_like(acc)

    def count(i, carry):
        s = i // per_src
        sl = pl.ds(pl.multiple_of((i % per_src) * chunk, chunk), chunk)
        slot = slot_ref[s, :, sl]
        g = g_ref[s, :, sl].astype(jnp.float32)
        cols = jnp.concatenate(
            [jnp.where(slot == float(q), g, 0.0) for q in range(pcount)], axis=0
        ).astype(jnp.bfloat16)
        for f in range(f_own):
            onehot = jnp.where(
                bins_ref[s, f:f + 1, sl] == iota, jnp.bfloat16(1), jnp.bfloat16(0))
            acc[f] += lax.dot_general(cols, onehot, NT, preferred_element_type=jnp.float32)
        return carry

    lax.fori_loop(0, n_src * per_src, count, 0)

    upper = (
        lax.broadcasted_iota(jnp.int32, (levels, levels), 0)
        <= lax.broadcasted_iota(jnp.int32, (levels, levels), 1)
    ).astype(jnp.bfloat16)

    def finish(q, carry):
        flag = flag_ref[q]
        small = acc[:, pl.ds(pl.multiple_of(q * kc, kc), kc), :]
        parent = jnp.concatenate([pg_ref[q], ph_ref[q]], axis=1)
        sib = parent - small
        for child, n in ((small, 2 * q + flag), (sib, 2 * q + 1 - flag)):
            cg_ref[n] = child[:, :c_dev]
            ch_ref[n] = child[:, c_dev:]
            flat = child.reshape(f_own * kc, levels)
            left = sum(
                lax.dot_general(p, upper, NN, preferred_element_type=jnp.float32)
                for p in split3(flat)
            ).reshape(f_own, kc, levels)
            lg, lh = left[:, :c_dev], left[:, c_dev:]
            wg, wh = lg[:, :, levels - 1:], lh[:, :, levels - 1:]
            score = leaf_term(lg, lh) + leaf_term(wg - lg, wh - lh) - leaf_term(wg, wh)
            gain_ref[n] = jnp.sum(score, axis=1)
        return carry

    lax.fori_loop(0, pcount, finish, 0)


def gain_kernel(
    part_ref, gains_ref, best_ref,
    inbox, tops, r_send, r_recv, a_send, a_recv, m_send, m_recv, z_send, z_recv,
):
    n_row = lax.axis_size("rows")
    n_cls = lax.axis_size("cls")
    n_feat = lax.axis_size("feat")
    me_r = lax.axis_index("rows")
    me_c = lax.axis_index("cls")
    me_f = lax.axis_index("feat")
    nodes = part_ref.shape[0]
    share = nodes // n_cls
    lanes = best_ref.shape[1]

    barrier = pltpu.get_barrier_semaphore()
    for k in range(1, n_cls):
        pl.semaphore_signal(barrier, inc=1, device_id={"cls": lax.rem(me_c + k, n_cls)})
    for k in range(1, n_row):
        pl.semaphore_signal(barrier, inc=1, device_id={"rows": lax.rem(me_r + k, n_row)})
    for k in range(1, n_feat):
        pl.semaphore_signal(barrier, inc=1, device_id={"feat": lax.rem(me_f + k, n_feat)})
    pl.semaphore_wait(barrier, n_cls + n_row + n_feat - 3)

    first = []
    for k in range(1, n_cls):
        peer = lax.rem(me_c + k, n_cls)
        first.append(pltpu.make_async_remote_copy(
            src_ref=part_ref.at[pl.ds(peer * share, share)], dst_ref=inbox.at[k],
            send_sem=r_send.at[k], recv_sem=r_recv.at[k], device_id={"cls": peer}))
        first[-1].start()
    for c in first:
        c.wait_recv()
    mine = part_ref[pl.ds(me_c * share, share)]
    for k in range(1, n_cls):
        mine = mine + inbox[k]
    mine = mine * (1.0 / (4 * n_cls))
    gains_ref[pl.ds(me_c * share, share)] = mine
    second = []
    for k in range(1, n_cls):
        peer = lax.rem(me_c + k, n_cls)
        own = pl.ds(me_c * share, share)
        second.append(pltpu.make_async_remote_copy(
            src_ref=gains_ref.at[own], dst_ref=gains_ref.at[own],
            send_sem=a_send.at[k], recv_sem=a_recv.at[k], device_id={"cls": peer}))
        second[-1].start()
    for c in second:
        c.wait()

    full = gains_ref[...]
    top = jnp.max(jnp.maximum(full[:, :, :lanes], full[:, :, lanes:]), axis=1)
    top = jnp.concatenate([top] * (lanes // nodes), axis=0)
    local = jnp.max(jnp.transpose(top), axis=0, keepdims=True)
    tops[0] = local
    third = []
    for k in range(1, n_feat):
        third.append(pltpu.make_async_remote_copy(
            src_ref=tops.at[0], dst_ref=tops.at[k],
            send_sem=m_send.at[k], recv_sem=m_recv.at[k],
            device_id={"feat": lax.rem(me_f + k, n_feat)}))
        third[-1].start()
    for c in third:
        c.wait()
    for k in range(1, n_feat):
        local = jnp.maximum(local, tops[k])
    tops[n_feat] = local
    fourth = []
    for k in range(1, n_row):
        fourth.append(pltpu.make_async_remote_copy(
            src_ref=tops.at[n_feat], dst_ref=tops.at[n_feat + k],
            send_sem=z_send.at[k], recv_sem=z_recv.at[k],
            device_id={"rows": lax.rem(me_r + k, n_row)}))
        fourth[-1].start()
    for c in fourth:
        c.wait()
    for k in range(1, n_row):
        local = jnp.maximum(local, tops[n_feat + k])
    best_ref[...] = local
    for c in first:
        c.wait_send()


def per_device(bins, logits, labels, node_ids, small_flag, parent_grad, parent_hess):
    n_row = lax.axis_size("rows")
    n_cls = lax.axis_size("cls")
    n_feat = lax.axis_size("feat")
    rows_here, c_dev = logits.shape
    pcount, f_own, _, levels = parent_grad.shape
    nodes = 2 * pcount
    vmem = pl.BlockSpec(memory_space=pltpu.VMEM)
    smem = pl.BlockSpec(memory_space=pltpu.SMEM)
    dma = pltpu.SemaphoreType.DMA

    allbins, allslot, allg = pl.pallas_call(
        exchange_kernel,
        out_shape=(
            jax.ShapeDtypeStruct((n_row, f_own, rows_here), jnp.bfloat16),
            jax.ShapeDtypeStruct((n_row, 1, rows_here), jnp.float32),
            jax.ShapeDtypeStruct((n_row, 2 * c_dev, rows_here), jnp.bfloat16),
        ),
        in_specs=[vmem, vmem, vmem, vmem, smem],
        out_specs=(vmem, vmem, vmem),
        scratch_shapes=[
            pltpu.VMEM((n_row, f_own, rows_here), jnp.bfloat16),
            pltpu.VMEM((n_cls, 2, rows_here), jnp.float32),
            dma((n_row,)), dma((n_row,)), dma((n_row,)), dma((n_row,)),
            dma((n_cls,)), dma((n_cls,)), dma((n_row,)), dma((n_row,)),
        ],
        compiler_params=pltpu.CompilerParams(
            collective_id=0, has_side_effects=True, vmem_limit_bytes=32 << 20),
        name="exchange_rows",
    )(bins, logits, labels.reshape(1, rows_here), node_ids.reshape(1, rows_here), small_flag)

    child_grad, child_hess, part = pl.pallas_call(
        level_kernel,
        out_shape=(
            jax.ShapeDtypeStruct((nodes, f_own, c_dev, levels), jnp.float32),
            jax.ShapeDtypeStruct((nodes, f_own, c_dev, levels), jnp.float32),
            jax.ShapeDtypeStruct((nodes, f_own, levels), jnp.float32),
        ),
        in_specs=[vmem, vmem, vmem, smem, vmem, vmem],
        out_specs=(vmem, vmem, vmem),
        scratch_shapes=[pltpu.VMEM((f_own, pcount * 2 * c_dev, levels), jnp.float32)],
        compiler_params=pltpu.CompilerParams(vmem_limit_bytes=48 << 20),
        name="level_scores",
    )(allbins, allslot, allg, small_flag, parent_grad, parent_hess)

    gains, best = pl.pallas_call(
        gain_kernel,
        out_shape=(
            jax.ShapeDtypeStruct((nodes, f_own, levels), jnp.float32),
            jax.ShapeDtypeStruct((1, 128), jnp.float32),
        ),
        in_specs=[vmem],
        out_specs=(vmem, vmem),
        scratch_shapes=[
            pltpu.VMEM((n_cls, nodes // n_cls, f_own, levels), jnp.float32),
            pltpu.VMEM((n_feat + n_row, 1, 128), jnp.float32),
            dma((n_cls,)), dma((n_cls,)), dma((n_cls,)), dma((n_cls,)),
            dma((n_feat,)), dma((n_feat,)), dma((n_row,)), dma((n_row,)),
        ],
        compiler_params=pltpu.CompilerParams(
            collective_id=1, has_side_effects=True, vmem_limit_bytes=32 << 20),
        name="combine_gains",
    )(part)
    return child_grad, child_hess, gains, best[0, :nodes]


def solution(mesh):
    in_specs = (
        P("rows", "feat"),
        P("rows", "cls"),
        P("rows"),
        P("rows"),
        P(),
        P(None, ("feat", "rows"), "cls", None),
        P(None, ("feat", "rows"), "cls", None),
    )
    out_specs = (
        P(None, ("feat", "rows"), "cls", None),
        P(None, ("feat", "rows"), "cls", None),
        P(None, ("feat", "rows"), None),
        P(),
    )
    return jax.shard_map(
        per_device, mesh=mesh, in_specs=in_specs, out_specs=out_specs, check_vma=False
    )
```

```python
import functools

import jax
import jax.numpy as jnp
from jax import lax
from jax.experimental import pallas as pl
from jax.experimental.pallas import tpu as pltpu
from jax.sharding import PartitionSpec as P

ridge_weight = 1.0
NN = (((1,), (0,)), ((), ()))


def leaf_term(grad_sum, hess_sum):
    return grad_sum * grad_sum / (jnp.maximum(hess_sum, 0.0) + ridge_weight)


def level_kernel(
    bins_hbm, logits_hbm, labels_hbm, node_hbm, flag_hbm, pg_hbm, ph_hbm,
    cg_hbm, ch_hbm, gains_hbm, best_ref,
    cg_ref, ch_ref, gains_ref, out_sem, bins_ref, logits_ref, labels_ref, node_ref, flag_ref, pg_ref, ph_ref, load_sem,
    sendb, bins_in, slot_in, g_in, stats, acc, part, inbox, tops, peaks,
    b_send, b_recv, s_send, s_recv, t_send, t_recv, g_send, g_recv,
    r_send, r_recv, a_send, a_recv, m_send, m_recv, z_send, z_recv,
):
    n_row = lax.axis_size("rows")
    n_cls = lax.axis_size("cls")
    n_feat = lax.axis_size("feat")
    me_r = lax.axis_index("rows")
    me_c = lax.axis_index("cls")
    me_f = lax.axis_index("feat")
    pcount, f_own, c_dev, levels = pg_ref.shape
    rows_here = node_ref.shape[1]
    kc = 2 * c_dev
    nodes = 2 * pcount
    share = nodes // n_cls
    n_grid = n_row * n_feat
    near = [k for pair in zip(range(1, n_row // 2), range(n_row - 1, n_row // 2, -1)) for k in pair]
    near = near + [n_row // 2]

    def peer_of(axis, k):
        size = lax.axis_size(axis)
        return {axis: lax.rem(lax.axis_index(axis) + k, size)}

    loads = [
        pltpu.make_async_copy(src, dst, load_sem.at[i])
        for i, (src, dst) in enumerate((
            (flag_hbm, flag_ref), (node_hbm, node_ref), (bins_hbm, bins_ref),
            (logits_hbm, logits_ref), (labels_hbm, labels_ref),
            (pg_hbm, pg_ref), (ph_hbm, ph_ref)))
    ]
    for c in loads:
        c.start()

    barrier = pltpu.get_barrier_semaphore()
    for axis, size in (("cls", n_cls), ("rows", n_row), ("feat", n_feat)):
        for k in range(1, size):
            pl.semaphore_signal(barrier, inc=1, device_id=peer_of(axis, k))

    loads[3].wait()
    lt = logits_ref[...]
    top = jnp.max(lt, axis=0, keepdims=True)
    exps = jnp.sum(jnp.exp(lt - top), axis=0, keepdims=True)
    stats[0] = jnp.concatenate([top, exps], axis=0)
    pl.semaphore_wait(barrier, n_cls + n_row + n_feat - 3)

    def stat_copy(k):
        return pltpu.make_async_remote_copy(
            src_ref=stats.at[0], dst_ref=stats.at[k],
            send_sem=t_send.at[k], recv_sem=t_recv.at[k],
            device_id={"cls": lax.rem(me_c + k, n_cls)})

    def bins_copy(k):
        peer = lax.rem(me_r + k, n_row)
        return pltpu.make_async_remote_copy(
            src_ref=sendb.at[peer], dst_ref=bins_in.at[k],
            send_sem=b_send.at[k], recv_sem=b_recv.at[k], device_id={"rows": peer})

    def slot_copy(k):
        return pltpu.make_async_remote_copy(
            src_ref=slot_in.at[0], dst_ref=slot_in.at[k],
            send_sem=s_send.at[k], recv_sem=s_recv.at[k],
            device_id={"rows": lax.rem(me_r + k, n_row)})

    def grad_copy(k):
        return pltpu.make_async_remote_copy(
            src_ref=g_in.at[0], dst_ref=g_in.at[k],
            send_sem=g_send.at[k], recv_sem=g_recv.at[k],
            device_id={"rows": lax.rem(me_r + k, n_row)})

    for k in range(1, n_cls):
        stat_copy(k).start()
    loads[2].wait()
    sendb[...] = bins_ref[...].astype(jnp.float32).astype(jnp.bfloat16).reshape(
        n_row, f_own, rows_here)
    for k in near:
        bins_copy(k).start()
    bins_in[0] = sendb[me_r]
    loads[0].wait()
    loads[1].wait()
    loads[4].wait()
    node = node_ref[...]
    slot = jnp.full(node.shape, -1.0, jnp.float32)
    for q in range(pcount):
        slot = jnp.where(node == 2 * q + flag_ref[q], float(q), slot)
    slot_in[0] = slot
    for k in near:
        slot_copy(k).start()
    for k in range(1, n_cls):
        stat_copy(k).wait_recv()
    heads = [stats[d, 0:1, :] for d in range(n_cls)]
    peak = functools.reduce(jnp.maximum, heads)
    denom = functools.reduce(
        jnp.add, [stats[d, 1:2, :] * jnp.exp(heads[d] - peak) for d in range(n_cls)])
    likely = jnp.exp(lt - peak) / denom
    classes = me_c * c_dev + lax.broadcasted_iota(jnp.int32, lt.shape, 0)
    target = (labels_ref[...] == classes).astype(jnp.float32)
    both = jnp.concatenate([likely - target, likely * (1.0 - likely)], axis=0)
    g_in[0] = both.astype(jnp.bfloat16)
    for k in near:
        grad_copy(k).start()

    iota = lax.broadcasted_iota(jnp.int32, (rows_here, levels), 1).astype(jnp.bfloat16)

    def count(group, first):
        cols, by_row = [], []
        for k in group:
            g = g_in[k].astype(jnp.float32)
            slot = jnp.broadcast_to(slot_in[k], (kc, rows_here))
            cols.append(jnp.concatenate(
                [jnp.where(slot == float(q), g, 0.0) for q in range(pcount)], axis=0
            ).astype(jnp.bfloat16))
            by_row.append(jnp.transpose(bins_in[k].astype(jnp.float32)).astype(jnp.bfloat16))
        cols = jnp.concatenate(cols, axis=1)
        for f in range(f_own):
            onehot = jnp.concatenate([
                jnp.where(
                    jnp.broadcast_to(b[:, f:f + 1], (rows_here, levels)) == iota,
                    jnp.bfloat16(1), jnp.bfloat16(0))
                for b in by_row
            ], axis=0)
            found = lax.dot_general(cols, onehot, NN, preferred_element_type=jnp.float32)
            if first:
                acc[f] = found
            else:
                acc[f] += found

    count([0], True)
    groups = [near[:2], near[2:4], near[4:]]
    for group in groups:
        for k in group:
            bins_copy(k).wait_recv()
            slot_copy(k).wait_recv()
            grad_copy(k).wait_recv()
        count(group, False)

    for c in loads[5:]:
        c.wait()
    upper = (
        lax.broadcasted_iota(jnp.int32, (levels, levels), 0)
        <= lax.broadcasted_iota(jnp.int32, (levels, levels), 1)
    ).astype(jnp.bfloat16)

    def small_and_sibling(q):
        small = acc[:, pl.ds(pl.multiple_of(q * kc, kc), kc), :]
        small_g, small_h = small[:, :c_dev], small[:, c_dev:]
        return small_g, small_h, pg_ref[q] - small_g, ph_ref[q] - small_h

    per_owner = share // 2
    flat_rows = f_own * kc
    out_rows = per_owner * 2 * f_own
    col = lax.broadcasted_iota(jnp.int32, (out_rows, 2 * per_owner * flat_rows), 1)
    row = lax.broadcasted_iota(jnp.int32, (out_rows, 2 * per_owner * flat_rows), 0)
    group_of_col = lax.rem(col, per_owner * flat_rows) // c_dev
    group_of_row = (row // (2 * f_own)) * 2 * f_own + 2 * lax.rem(row, f_own) + lax.rem(
        row // f_own, 2)
    over_classes = (group_of_col == group_of_row).astype(jnp.bfloat16)

    def two_parts(x):
        hi = x.astype(jnp.bfloat16)
        low = (x - hi.astype(jnp.float32)).astype(jnp.bfloat16)
        return jnp.concatenate([hi, low], axis=0)

    def scores(first_q):
        flat_g, flat_h = [], []
        for i in range(per_owner):
            small_g, small_h, sib_g, sib_h = small_and_sibling(first_q + i)
            flat_g.append(jnp.concatenate([small_g, sib_g], axis=1).reshape(flat_rows, levels))
            flat_h.append(jnp.concatenate([small_h, sib_h], axis=1).reshape(flat_rows, levels))
        flat = jnp.concatenate(flat_g + flat_h, axis=0)
        size = flat.shape[0]
        left = lax.dot_general(two_parts(flat), upper, NN, preferred_element_type=jnp.float32)
        left = left[:size] + left[size:]
        lg, lh = left[:size // 2], left[size // 2:]
        wg, wh = lg[:, levels - 1:], lh[:, levels - 1:]
        term = leaf_term(lg, lh) + leaf_term(wg - lg, wh - lh) - leaf_term(wg, wh)
        sums = lax.dot_general(
            over_classes, two_parts(term), NN, preferred_element_type=jnp.float32)
        for i in range(per_owner):
            q = first_q + i
            zero = flag_ref[q] == 0
            small = sums[(2 * i) * f_own:(2 * i + 1) * f_own]
            sib = sums[(2 * i + 1) * f_own:(2 * i + 2) * f_own]
            part[2 * q] = jnp.where(zero, small, sib)
            part[2 * q + 1] = jnp.where(zero, sib, small)

    def part_copy(j):
        peer = lax.rem(me_c + j, n_cls)
        return pltpu.make_async_remote_copy(
            src_ref=part.at[pl.ds(peer * share, share)], dst_ref=inbox.at[j],
            send_sem=r_send.at[j], recv_sem=r_recv.at[j], device_id={"cls": peer})

    def partial_gains(j, carry):
        owner = lax.rem(me_c + j, n_cls)

        scores(owner * per_owner)

        @pl.when(j < n_cls)
        def _():
            part_copy(j).start()

        return carry

    lax.fori_loop(1, n_cls + 1, partial_gains, 0)

    own = pl.ds(me_c * share, share)
    mine = part[own]
    for j in range(1, n_cls):
        part_copy(j).wait_recv()
        mine = mine + inbox[j]
    mine = mine * (1.0 / (c_dev * n_cls))
    gains_ref[own] = mine

    def full_copy(k):
        return pltpu.make_async_remote_copy(
            src_ref=gains_ref.at[own], dst_ref=gains_ref.at[own],
            send_sem=a_send.at[k], recv_sem=a_recv.at[k],
            device_id={"cls": lax.rem(me_c + k, n_cls)})

    lanes = levels // 2
    tops[0] = jnp.max(jnp.maximum(mine[:, :, :lanes], mine[:, :, lanes:]), axis=1)

    def top_copy(k):
        spot = lax.rem(me_f * n_row + me_r + k, n_grid)
        return pltpu.make_async_remote_copy(
            src_ref=tops.at[0], dst_ref=tops.at[k],
            send_sem=m_send.at[k], recv_sem=m_recv.at[k],
            device_id={"rows": lax.rem(spot, n_row), "feat": spot // n_row})

    def peak_copy(k):
        return pltpu.make_async_remote_copy(
            src_ref=peaks.at[me_c], dst_ref=peaks.at[me_c],
            send_sem=z_send.at[k], recv_sem=z_recv.at[k],
            device_id={"cls": lax.rem(me_c + k, n_cls)})

    for k in range(1, n_grid):
        top_copy(k).start()
    for k in range(1, n_cls):
        full_copy(k).start()

    def write(q, carry):
        small_g, small_h, sib_g, sib_h = small_and_sibling(q)
        zero = flag_ref[q] == 0
        cg_ref[2 * q] = jnp.where(zero, small_g, sib_g)
        ch_ref[2 * q] = jnp.where(zero, small_h, sib_h)
        cg_ref[2 * q + 1] = jnp.where(zero, sib_g, small_g)
        ch_ref[2 * q + 1] = jnp.where(zero, sib_h, small_h)
        return carry

    lax.fori_loop(0, pcount, write, 0)
    stores = [
        pltpu.make_async_copy(cg_ref, cg_hbm, out_sem.at[0]),
        pltpu.make_async_copy(ch_ref, ch_hbm, out_sem.at[1]),
    ]
    for c in stores:
        c.start()

    highest = tops[0]
    for k in range(1, n_grid):
        top_copy(k).wait_recv()
        highest = jnp.maximum(highest, tops[k])
    peaks[me_c] = highest
    for k in range(1, n_cls):
        peak_copy(k).start()
    for k in range(1, n_cls):
        full_copy(k).wait_recv()
    stores.append(pltpu.make_async_copy(gains_ref, gains_hbm, out_sem.at[2]))
    stores[-1].start()
    for k in range(1, n_cls):
        peak_copy(k).wait_recv()
    table = peaks[...].reshape(nodes, lanes)
    table = jnp.concatenate([table] * (lanes // nodes), axis=0)
    best_ref[...] = jnp.max(jnp.transpose(table), axis=0, keepdims=True)[:, :nodes]

    for c in stores:
        c.wait()
    for k in range(1, n_cls):
        full_copy(k).wait_send()
        stat_copy(k).wait_send()
        part_copy(k).wait_send()
        peak_copy(k).wait_send()
    for k in range(1, n_row):
        bins_copy(k).wait_send()
        slot_copy(k).wait_send()
        grad_copy(k).wait_send()
    for k in range(1, n_grid):
        top_copy(k).wait_send()


def store_kernel(cg, ch, gains, best, cg_out, ch_out, gains_out, best_out, *scratch):
    held, (in_sem, out_sem) = scratch[:4], scratch[4:]
    moves = []
    for src, via, dst in zip((cg, ch, gains, best), held, (cg_out, ch_out, gains_out, best_out)):
        pieces = 4 if src.shape[0] % 4 == 0 and len(src.shape) == 4 else 1
        size = src.shape[0] // pieces
        for p in range(pieces):
            moves.append([r.at[pl.ds(p * size, size)] for r in (src, via, dst)])
    first = [pltpu.make_async_copy(m[0], m[1], in_sem.at[i]) for i, m in enumerate(moves)]
    second = [pltpu.make_async_copy(m[1], m[2], out_sem.at[i]) for i, m in enumerate(moves)]
    for c in first:
        c.start()
    for a, b in zip(first, second):
        a.wait()
        b.start()
    for c in second:
        c.wait()


def per_device(bins, logits, labels, node_ids, small_flag, parent_grad, parent_hess):
    n_row = lax.axis_size("rows")
    n_cls = lax.axis_size("cls")
    n_grid = n_row * lax.axis_size("feat")
    rows_here, c_dev = logits.shape
    pcount, f_own, _, levels = parent_grad.shape
    nodes = 2 * pcount
    share = nodes // n_cls
    kc = 2 * c_dev
    lanes = levels // 2
    vmem = pl.BlockSpec(memory_space=pltpu.VMEM)
    hbm = pl.BlockSpec(memory_space=pltpu.HBM)
    dma = pltpu.SemaphoreType.DMA
    f32, bf16 = jnp.float32, jnp.bfloat16

    child_grad, child_hess, gains, best = pl.pallas_call(
        level_kernel,
        out_shape=(
            jax.ShapeDtypeStruct((nodes, f_own, c_dev, levels), f32),
            jax.ShapeDtypeStruct((nodes, f_own, c_dev, levels), f32),
            jax.ShapeDtypeStruct((nodes, f_own, levels), f32),
            jax.ShapeDtypeStruct((1, nodes), f32),
        ),
        in_specs=[hbm] * 7,
        out_specs=(hbm, hbm, hbm, vmem),
        scratch_shapes=[
            pltpu.VMEM((nodes, f_own, c_dev, levels), f32),
            pltpu.VMEM((nodes, f_own, c_dev, levels), f32),
            pltpu.VMEM((nodes, f_own, levels), f32),
            dma((3,)),
            pltpu.VMEM((n_row * f_own, rows_here), jnp.int32),
            pltpu.VMEM((c_dev, rows_here), f32),
            pltpu.VMEM((1, rows_here), jnp.int32),
            pltpu.VMEM((1, rows_here), jnp.int32),
            pltpu.SMEM((pcount,), jnp.int32),
            pltpu.VMEM(parent_grad.shape, f32),
            pltpu.VMEM(parent_hess.shape, f32),
            dma((7,)),
            pltpu.VMEM((n_row, f_own, rows_here), bf16),
            pltpu.VMEM((n_row, f_own, rows_here), bf16),
            pltpu.VMEM((n_row, 1, rows_here), f32),
            pltpu.VMEM((n_row, kc, rows_here), bf16),
            pltpu.VMEM((n_cls, 2, rows_here), f32),
            pltpu.VMEM((f_own, pcount * kc, levels), f32),
            pltpu.VMEM((nodes, f_own, levels), f32),
            pltpu.VMEM((n_cls, share, f_own, levels), f32),
            pltpu.VMEM((n_grid, share, lanes), f32),
            pltpu.VMEM((n_cls, share, lanes), f32),
            dma((n_row,)), dma((n_row,)), dma((n_row,)), dma((n_row,)),
            dma((n_cls,)), dma((n_cls,)), dma((n_row,)), dma((n_row,)),
            dma((n_cls,)), dma((n_cls,)), dma((n_cls,)), dma((n_cls,)),
            dma((n_grid,)), dma((n_grid,)), dma((n_cls,)), dma((n_cls,)),
        ],
        compiler_params=pltpu.CompilerParams(
            collective_id=0, has_side_effects=True, vmem_limit_bytes=60 << 20),
        name="level_step",
    )(
        bins.T, logits.T, labels.reshape(1, rows_here), node_ids.reshape(1, rows_here),
        small_flag, parent_grad, parent_hess,
    )
    results = (child_grad, child_hess, gains, best)
    child_grad, child_hess, gains, best = pl.pallas_call(
        store_kernel,
        out_shape=tuple(jax.ShapeDtypeStruct(r.shape, r.dtype) for r in results),
        in_specs=[hbm] * 4,
        out_specs=(hbm,) * 4,
        scratch_shapes=[pltpu.VMEM(r.shape, r.dtype) for r in results] + [dma((10,)), dma((10,))],
        compiler_params=pltpu.CompilerParams(vmem_limit_bytes=60 << 20),
        name="store_results",
    )(*results)
    return child_grad, child_hess, gains, best.reshape(nodes)


def solution(mesh):
    in_specs = (
        P("rows", "feat"),
        P("rows", "cls"),
        P("rows"),
        P("rows"),
        P(),
        P(None, ("feat", "rows"), "cls", None),
        P(None, ("feat", "rows"), "cls", None),
    )
    out_specs = (
        P(None, ("feat", "rows"), "cls", None),
        P(None, ("feat", "rows"), "cls", None),
        P(None, ("feat", "rows"), None),
        P(),
    )
    return jax.shard_map(
        per_device, mesh=mesh, in_specs=in_specs, out_specs=out_specs, check_vma=False
    )
```

```python
import functools

import jax
import jax.numpy as jnp
from jax import lax
from jax.experimental import pallas as pl
from jax.experimental.pallas import tpu as pltpu
from jax.sharding import PartitionSpec as P

ridge_weight = 1.0
NN = (((1,), (0,)), ((), ()))


def leaf_term(grad_sum, hess_sum):
    return grad_sum * grad_sum / (jnp.maximum(hess_sum, 0.0) + ridge_weight)


def level_kernel(
    bins_hbm, logits_hbm, labels_hbm, node_hbm, flag_hbm, pg_hbm, ph_hbm,
    cg_hbm, ch_hbm, gains_hbm, best_ref,
    cg_ref, ch_ref, gains_ref, out_sem, bins_ref, logits_ref, labels_ref, node_ref, flag_ref, pg_ref, ph_ref, load_sem,
    sendb, bins_in, g_in, stats, acc, part, inbox, tops, peaks,
    b_send, b_recv, t_send, t_recv, g_send, g_recv,
    r_send, r_recv, a_send, a_recv, m_send, m_recv, z_send, z_recv,
):
    n_row = lax.axis_size("rows")
    n_cls = lax.axis_size("cls")
    n_feat = lax.axis_size("feat")
    me_r = lax.axis_index("rows")
    me_c = lax.axis_index("cls")
    me_f = lax.axis_index("feat")
    pcount, f_own, c_dev, levels = pg_ref.shape
    rows_here = labels_ref.shape[1]
    kc = 2 * c_dev
    nodes = 2 * pcount
    share = nodes // n_cls
    n_x = n_cls // 2
    n_core = n_feat // 2
    half = rows_here // 128 // 2
    near = [k for pair in zip(range(1, n_row // 2), range(n_row - 1, n_row // 2, -1)) for k in pair]
    near = near + [n_row // 2]

    far = near[::-1]
    ring_x = [n_x // 2] + [d for i in range(1, n_x // 2) for d in (i, n_x - i)]
    cls_steps = [(1, d) for d in ring_x + [0]] + [(0, d) for d in ring_x]
    grid_steps = [(d, e) for d in far for e in range(n_core)] + [
        (0, e) for e in range(1, n_core)]
    wide_steps = [(1, c) for c in cls_steps + [(0, 0)]] + [(0, c) for c in cls_steps]

    def peer_of(axis, k):
        size = lax.axis_size(axis)
        return {axis: lax.rem(lax.axis_index(axis) + k, size)}

    def cls_peer(step):
        dy, dx = step
        return lax.rem(me_c // n_x + dy, 2) * n_x + lax.rem(lax.rem(me_c, n_x) + dx, n_x)

    def grid_peer(step):
        dr, dc = step
        core = lax.rem(lax.rem(me_f, n_core) + dc, n_core)
        return {"rows": lax.rem(me_r + dr, n_row), "feat": me_f // n_core * n_core + core}

    def wide_peer(step):
        dl, c = step
        low = lax.rem(me_f // n_core + dl, 2)
        return {"cls": cls_peer(c), "feat": low * n_core + lax.rem(me_f, n_core)}

    loads = [
        pltpu.make_async_copy(src, dst, load_sem.at[i])
        for i, (src, dst) in enumerate((
            (flag_hbm, flag_ref), (node_hbm, node_ref), (bins_hbm, bins_ref),
            (logits_hbm, logits_ref), (labels_hbm, labels_ref),
            (pg_hbm, pg_ref), (ph_hbm, ph_ref)))
    ]
    for c in loads:
        c.start()

    barrier = pltpu.get_barrier_semaphore()
    for axis, size in (("cls", n_cls), ("rows", n_row), ("feat", n_feat)):
        for k in range(1, size):
            pl.semaphore_signal(barrier, inc=1, device_id=peer_of(axis, k))

    loads[3].wait()
    lt = logits_ref[...]
    top = jnp.max(lt, axis=0, keepdims=True)
    exps = jnp.sum(jnp.exp(lt - top), axis=0, keepdims=True)
    stats[0] = jnp.concatenate([top, exps], axis=0)
    pl.semaphore_wait(barrier, n_cls + n_row + n_feat - 3)

    def stat_copy(k):
        return pltpu.make_async_remote_copy(
            src_ref=stats.at[0], dst_ref=stats.at[k],
            send_sem=t_send.at[k], recv_sem=t_recv.at[k],
            device_id={"cls": cls_peer(cls_steps[k - 1])})

    def bins_copy(k):
        peer = lax.rem(me_r + k, n_row)
        return pltpu.make_async_remote_copy(
            src_ref=sendb.at[peer], dst_ref=bins_in.at[k],
            send_sem=b_send.at[k], recv_sem=b_recv.at[k], device_id={"rows": peer})

    def grad_copy(k):
        return pltpu.make_async_remote_copy(
            src_ref=g_in.at[0], dst_ref=g_in.at[k],
            send_sem=g_send.at[k], recv_sem=g_recv.at[k],
            device_id={"rows": lax.rem(me_r + k, n_row)})

    for k in range(1, n_cls):
        stat_copy(k).start()
    for c in loads[:3]:
        c.wait()
    node = node_ref[...]
    slot = jnp.full(node.shape, -1.0, jnp.float32)
    for q in range(pcount):
        slot = jnp.where(node == 2 * q + flag_ref[q], float(q), slot)
    tail = jnp.concatenate([slot[:half], slot[half:]], axis=1).astype(jnp.bfloat16)
    sendb[:, :, :rows_here] = bins_ref[...].astype(jnp.float32).astype(jnp.bfloat16).reshape(
        n_row, f_own, rows_here)
    for d in range(n_row):
        sendb[d, :, rows_here:] = tail
    for k in near:
        bins_copy(k).start()
    bins_in[0] = sendb[me_r]
    loads[4].wait()
    for k in range(1, n_cls):
        stat_copy(k).wait_recv()
    heads = [stats[d, 0:1, :] for d in range(n_cls)]
    peak = functools.reduce(jnp.maximum, heads)
    denom = functools.reduce(
        jnp.add, [stats[d, 1:2, :] * jnp.exp(heads[d] - peak) for d in range(n_cls)])
    likely = jnp.exp(lt - peak) / denom
    classes = me_c * c_dev + lax.broadcasted_iota(jnp.int32, lt.shape, 0)
    target = (labels_ref[...] == classes).astype(jnp.float32)
    both = jnp.concatenate([likely - target, likely * (1.0 - likely)], axis=0)
    g_in[0] = both.astype(jnp.bfloat16)
    for k in near:
        grad_copy(k).start()

    iota = lax.broadcasted_iota(jnp.int32, (rows_here, levels), 1).astype(jnp.bfloat16)

    def count(group, first):
        cols, by_row = [], []
        for k in group:
            g = g_in[k].astype(jnp.float32)
            tail = bins_in[k, :, rows_here:].astype(jnp.float32)
            slot = jnp.concatenate([
                jnp.broadcast_to(tail[i:i + 1, h * 128:(h + 1) * 128], (kc, 128))
                for h in range(2) for i in range(half)
            ], axis=1)
            cols.append(jnp.concatenate(
                [jnp.where(slot == float(q), g, 0.0) for q in range(pcount)], axis=0
            ).astype(jnp.bfloat16))
            by_row.append(jnp.transpose(bins_in[k, :, :rows_here].astype(jnp.float32)).astype(jnp.bfloat16))
        cols = jnp.concatenate(cols, axis=1)
        for f in range(f_own):
            onehot = jnp.concatenate([
                jnp.where(
                    jnp.broadcast_to(b[:, f:f + 1], (rows_here, levels)) == iota,
                    jnp.bfloat16(1), jnp.bfloat16(0))
                for b in by_row
            ], axis=0)
            found = lax.dot_general(cols, onehot, NN, preferred_element_type=jnp.float32)
            if first:
                acc[f] = found
            else:
                acc[f] += found

    count([0], True)
    groups = [near[:2], near[2:4], near[4:]]
    for group in groups:
        for k in group:
            bins_copy(k).wait_recv()
            grad_copy(k).wait_recv()
        count(group, False)

    for c in loads[5:]:
        c.wait()
    upper = (
        lax.broadcasted_iota(jnp.int32, (levels, levels), 0)
        <= lax.broadcasted_iota(jnp.int32, (levels, levels), 1)
    ).astype(jnp.bfloat16)

    def small_and_sibling(q):
        small = acc[:, pl.ds(pl.multiple_of(q * kc, kc), kc), :]
        small_g, small_h = small[:, :c_dev], small[:, c_dev:]
        return small_g, small_h, pg_ref[q] - small_g, ph_ref[q] - small_h

    per_owner = share // 2
    flat_rows = f_own * kc
    out_rows = per_owner * 2 * f_own
    col = lax.broadcasted_iota(jnp.int32, (out_rows, 2 * per_owner * flat_rows), 1)
    row = lax.broadcasted_iota(jnp.int32, (out_rows, 2 * per_owner * flat_rows), 0)
    group_of_col = lax.rem(col, per_owner * flat_rows) // c_dev
    group_of_row = (row // (2 * f_own)) * 2 * f_own + 2 * lax.rem(row, f_own) + lax.rem(
        row // f_own, 2)
    over_classes = (group_of_col == group_of_row).astype(jnp.bfloat16)

    def two_parts(x):
        hi = x.astype(jnp.bfloat16)
        low = (x - hi.astype(jnp.float32)).astype(jnp.bfloat16)
        return jnp.concatenate([hi, low], axis=0)

    def scores(first_q):
        flat_g, flat_h = [], []
        for i in range(per_owner):
            small_g, small_h, sib_g, sib_h = small_and_sibling(first_q + i)
            flat_g.append(jnp.concatenate([small_g, sib_g], axis=1).reshape(flat_rows, levels))
            flat_h.append(jnp.concatenate([small_h, sib_h], axis=1).reshape(flat_rows, levels))
        flat = jnp.concatenate(flat_g + flat_h, axis=0)
        size = flat.shape[0]
        left = lax.dot_general(two_parts(flat), upper, NN, preferred_element_type=jnp.float32)
        left = left[:size] + left[size:]
        lg, lh = left[:size // 2], left[size // 2:]
        wg, wh = lg[:, levels - 1:], lh[:, levels - 1:]
        term = leaf_term(lg, lh) + leaf_term(wg - lg, wh - lh) - leaf_term(wg, wh)
        sums = lax.dot_general(
            over_classes, two_parts(term), NN, preferred_element_type=jnp.float32)
        for i in range(per_owner):
            q = first_q + i
            zero = flag_ref[q] == 0
            small = sums[(2 * i) * f_own:(2 * i + 1) * f_own]
            sib = sums[(2 * i + 1) * f_own:(2 * i + 2) * f_own]
            part[2 * q] = jnp.where(zero, small, sib)
            part[2 * q + 1] = jnp.where(zero, sib, small)

    def part_copy(j, peer):
        return pltpu.make_async_remote_copy(
            src_ref=part.at[pl.ds(peer * share, share)], dst_ref=inbox.at[j],
            send_sem=r_send.at[j], recv_sem=r_recv.at[j], device_id={"cls": peer})

    def partial_gains(j, carry):
        place = lax.rem(j, n_x)
        dx = jnp.where(place == 0, n_x // 2, jnp.where(place == n_x - 1, 0, 2 * place - 1))
        owner = cls_peer((jnp.where(j < n_x, 1, 0), dx))
        scores(owner * per_owner)

        @pl.when(j < n_cls - 1)
        def _():
            part_copy(j, owner).start()

        return carry

    lax.fori_loop(0, n_cls, partial_gains, 0)

    own = pl.ds(me_c * share, share)
    mine = part[own]
    for j in range(n_cls - 1):
        part_copy(j, cls_peer(cls_steps[j])).wait_recv()
        mine = mine + inbox[j]
    mine = mine * (1.0 / (c_dev * n_cls))
    gains_ref[own] = mine

    def full_copy(k):
        return pltpu.make_async_remote_copy(
            src_ref=gains_ref.at[own], dst_ref=gains_ref.at[own],
            send_sem=a_send.at[k], recv_sem=a_recv.at[k],
            device_id={"cls": cls_peer(cls_steps[k - 1])})

    lanes = levels // 2
    tops[0] = jnp.max(jnp.maximum(mine[:, :, :lanes], mine[:, :, lanes:]), axis=1)

    def top_copy(k):
        return pltpu.make_async_remote_copy(
            src_ref=tops.at[0], dst_ref=tops.at[k],
            send_sem=m_send.at[k], recv_sem=m_recv.at[k],
            device_id=grid_peer(grid_steps[k - 1]))

    me_low = me_f // n_core

    def peak_copy(k):
        return pltpu.make_async_remote_copy(
            src_ref=peaks.at[me_low, me_c], dst_ref=peaks.at[me_low, me_c],
            send_sem=z_send.at[k], recv_sem=z_recv.at[k],
            device_id=wide_peer(wide_steps[k - 1]))

    n_grid, n_wide = len(grid_steps) + 1, len(wide_steps) + 1
    for k in range(1, n_grid):
        top_copy(k).start()
    for k in range(1, n_cls):
        full_copy(k).start()

    def write(q, carry):
        small_g, small_h, sib_g, sib_h = small_and_sibling(q)
        zero = flag_ref[q] == 0
        cg_ref[2 * q] = jnp.where(zero, small_g, sib_g)
        ch_ref[2 * q] = jnp.where(zero, small_h, sib_h)
        cg_ref[2 * q + 1] = jnp.where(zero, sib_g, small_g)
        ch_ref[2 * q + 1] = jnp.where(zero, sib_h, small_h)
        return carry

    lax.fori_loop(0, pcount, write, 0)
    stores = [
        pltpu.make_async_copy(cg_ref, cg_hbm, out_sem.at[0]),
        pltpu.make_async_copy(ch_ref, ch_hbm, out_sem.at[1]),
    ]
    for c in stores:
        c.start()

    highest = tops[0]
    for k in range(1, n_grid):
        top_copy(k).wait_recv()
        highest = jnp.maximum(highest, tops[k])
    peaks[me_low, me_c] = jnp.broadcast_to(
        jnp.max(highest, axis=1, keepdims=True), highest.shape)
    for k in range(1, n_wide):
        peak_copy(k).start()
    for k in range(1, n_cls):
        full_copy(k).wait_recv()
    stores.append(pltpu.make_async_copy(gains_ref, gains_hbm, out_sem.at[2]))
    stores[-1].start()
    for k in range(1, n_wide):
        peak_copy(k).wait_recv()
    table = jnp.maximum(peaks[0], peaks[1]).reshape(nodes, lanes)
    diagonal = lax.broadcasted_iota(jnp.int32, table.shape, 0) == lax.broadcasted_iota(
        jnp.int32, table.shape, 1)
    best_ref[...] = jnp.max(
        jnp.where(diagonal, table, -jnp.inf), axis=0, keepdims=True)[:, :nodes]

    for c in stores:
        c.wait()
    for k in range(1, n_cls):
        full_copy(k).wait_send()
        stat_copy(k).wait_send()
        part_copy(k - 1, cls_peer(cls_steps[k - 1])).wait_send()
    for k in range(1, n_row):
        bins_copy(k).wait_send()
        grad_copy(k).wait_send()
    for k in range(1, n_grid):
        top_copy(k).wait_send()
    for k in range(1, n_wide):
        peak_copy(k).wait_send()


def store_kernel(cg, ch, gains, best, cg_out, ch_out, gains_out, best_out, *scratch):
    held, (in_sem, out_sem) = scratch[:4], scratch[4:]
    moves = []
    for src, via, dst in zip((cg, ch, gains, best), held, (cg_out, ch_out, gains_out, best_out)):
        pieces = 4 if src.shape[0] % 4 == 0 and len(src.shape) == 4 else 1
        size = src.shape[0] // pieces
        for p in range(pieces):
            moves.append([r.at[pl.ds(p * size, size)] for r in (src, via, dst)])
    first = [pltpu.make_async_copy(m[0], m[1], in_sem.at[i]) for i, m in enumerate(moves)]
    second = [pltpu.make_async_copy(m[1], m[2], out_sem.at[i]) for i, m in enumerate(moves)]
    for c in first:
        c.start()
    for a, b in zip(first, second):
        a.wait()
        b.start()
    for c in second:
        c.wait()


def per_device(bins, logits, labels, node_ids, small_flag, parent_grad, parent_hess):
    n_row = lax.axis_size("rows")
    n_cls = lax.axis_size("cls")
    n_grid = n_row * (lax.axis_size("feat") // 2)
    n_wide = 2 * n_cls
    rows_here, c_dev = logits.shape
    pcount, f_own, _, levels = parent_grad.shape
    nodes = 2 * pcount
    share = nodes // n_cls
    kc = 2 * c_dev
    lanes = levels // 2
    vmem = pl.BlockSpec(memory_space=pltpu.VMEM)
    hbm = pl.BlockSpec(memory_space=pltpu.HBM)
    dma = pltpu.SemaphoreType.DMA
    f32, bf16 = jnp.float32, jnp.bfloat16

    child_grad, child_hess, gains, best = pl.pallas_call(
        level_kernel,
        out_shape=(
            jax.ShapeDtypeStruct((nodes, f_own, c_dev, levels), f32),
            jax.ShapeDtypeStruct((nodes, f_own, c_dev, levels), f32),
            jax.ShapeDtypeStruct((nodes, f_own, levels), f32),
            jax.ShapeDtypeStruct((1, nodes), f32),
        ),
        in_specs=[hbm] * 7,
        out_specs=(hbm, hbm, hbm, vmem),
        scratch_shapes=[
            pltpu.VMEM((nodes, f_own, c_dev, levels), f32),
            pltpu.VMEM((nodes, f_own, c_dev, levels), f32),
            pltpu.VMEM((nodes, f_own, levels), f32),
            dma((3,)),
            pltpu.VMEM((n_row * f_own, rows_here), jnp.int32),
            pltpu.VMEM((c_dev, rows_here), f32),
            pltpu.VMEM((1, rows_here), jnp.int32),
            pltpu.VMEM((rows_here // 128, 128), jnp.int32),
            pltpu.SMEM((pcount,), jnp.int32),
            pltpu.VMEM(parent_grad.shape, f32),
            pltpu.VMEM(parent_hess.shape, f32),
            dma((7,)),
            pltpu.VMEM((n_row, f_own, rows_here + rows_here // f_own), bf16),
            pltpu.VMEM((n_row, f_own, rows_here + rows_here // f_own), bf16),
            pltpu.VMEM((n_row, kc, rows_here), bf16),
            pltpu.VMEM((n_cls, 2, rows_here), f32),
            pltpu.VMEM((f_own, pcount * kc, levels), f32),
            pltpu.VMEM((nodes, f_own, levels), f32),
            pltpu.VMEM((n_cls, share, f_own, levels), f32),
            pltpu.VMEM((n_grid, share, lanes), f32),
            pltpu.VMEM((2, n_cls, share, lanes), f32),
            dma((n_row,)), dma((n_row,)),
            dma((n_cls,)), dma((n_cls,)), dma((n_row,)), dma((n_row,)),
            dma((n_cls,)), dma((n_cls,)), dma((n_cls,)), dma((n_cls,)),
            dma((n_grid,)), dma((n_grid,)), dma((n_wide,)), dma((n_wide,)),
        ],
        compiler_params=pltpu.CompilerParams(
            collective_id=0, has_side_effects=True, vmem_limit_bytes=60 << 20),
        name="level_step",
    )(
        bins.T, logits.T, labels.reshape(1, rows_here), node_ids.reshape(rows_here // 128, 128),
        small_flag, parent_grad, parent_hess,
    )
    results = (child_grad, child_hess, gains, best)
    child_grad, child_hess, gains, best = pl.pallas_call(
        store_kernel,
        out_shape=tuple(jax.ShapeDtypeStruct(r.shape, r.dtype) for r in results),
        in_specs=[hbm] * 4,
        out_specs=(hbm,) * 4,
        scratch_shapes=[pltpu.VMEM(r.shape, r.dtype) for r in results] + [dma((10,)), dma((10,))],
        compiler_params=pltpu.CompilerParams(vmem_limit_bytes=60 << 20),
        name="store_results",
    )(*results)
    return child_grad, child_hess, gains, best.reshape(nodes)


def solution(mesh):
    in_specs = (
        P("rows", "feat"),
        P("rows", "cls"),
        P("rows"),
        P("rows"),
        P(),
        P(None, ("feat", "rows"), "cls", None),
        P(None, ("feat", "rows"), "cls", None),
    )
    out_specs = (
        P(None, ("feat", "rows"), "cls", None),
        P(None, ("feat", "rows"), "cls", None),
        P(None, ("feat", "rows"), None),
        P(),
    )
    return jax.shard_map(
        per_device, mesh=mesh, in_specs=in_specs, out_specs=out_specs, check_vma=False
    )
```

```python
import functools

import jax
import jax.numpy as jnp
from jax import lax
from jax.experimental import pallas as pl
from jax.experimental.pallas import tpu as pltpu
from jax.sharding import PartitionSpec as P

ridge_weight = 1.0
NN = (((1,), (0,)), ((), ()))


def leaf_term(grad_sum, hess_sum):
    return grad_sum * grad_sum / (jnp.maximum(hess_sum, 0.0) + ridge_weight)


def level_kernel(
    bins_hbm, logits_hbm, labels_hbm, node_hbm, flag_hbm, pg_hbm, ph_hbm,
    cg_hbm, ch_hbm, gains_hbm, best_ref,
    cg_ref, ch_ref, gains_ref, full, out_sem, bins_ref, logits_ref, labels_ref, node_ref, flag_ref, pg_ref, ph_ref, load_sem,
    sendb, bins_in, own_hot, g_in, stats, acc, part, inbox, tops, peaks,
    b_send, b_recv, t_send, t_recv, g_send, g_recv,
    r_send, r_recv, a_send, a_recv, m_send, m_recv, z_send, z_recv,
):
    n_row = lax.axis_size("rows")
    n_cls = lax.axis_size("cls")
    n_feat = lax.axis_size("feat")
    me_r = lax.axis_index("rows")
    me_c = lax.axis_index("cls")
    me_f = lax.axis_index("feat")
    pcount, f_own, c_dev, levels = pg_ref.shape
    rows_here = labels_ref.shape[1]
    assert f_own == n_cls
    kc = 2 * c_dev
    nodes = 2 * pcount
    share = nodes // n_cls
    n_x = n_cls // 2
    n_core = n_feat // 2
    half = rows_here // 128 // 2
    near = [k for pair in zip(range(1, n_row // 2), range(n_row - 1, n_row // 2, -1)) for k in pair]
    near = near + [n_row // 2]

    far = near[::-1]
    ring_x = [n_x // 2] + [d for i in range(1, n_x // 2) for d in (i, n_x - i)]
    cls_steps = [(1, d) for d in ring_x + [0]] + [(0, d) for d in ring_x]
    grid_steps = [(d, e) for d in far for e in range(n_core)] + [
        (0, e) for e in range(1, n_core)]
    wide_steps = [(1, c) for c in cls_steps + [(0, 0)]] + [(0, c) for c in cls_steps]

    me_x, me_y = lax.rem(me_c, n_x), me_c // n_x
    me_core, me_low = lax.rem(me_f, n_core), me_f // n_core

    def ahead(place, step, size):
        moved = place + step
        return jnp.where(moved >= size, moved - size, moved)

    def row_peer(k):
        return ahead(me_r, k, n_row)

    def cls_peer(step):
        dy, dx = step
        return ahead(me_y, dy, 2) * n_x + ahead(me_x, dx, n_x)

    def grid_peer(step):
        dr, dc = step
        return {
            "cls": me_c, "rows": row_peer(dr),
            "feat": me_low * n_core + ahead(me_core, dc, n_core)}

    def wide_peer(step):
        dl, c = step
        return {
            "cls": cls_peer(c), "rows": me_r,
            "feat": ahead(me_low, dl, 2) * n_core + me_core}

    def at_row(k):
        return {"rows": row_peer(k), "feat": me_f, "cls": me_c}

    def at_cls(k):
        return {"cls": cls_peer(cls_steps[k - 1]), "rows": me_r, "feat": me_f}

    loads = [
        pltpu.make_async_copy(src, dst, load_sem.at[i])
        for i, (src, dst) in enumerate((
            (flag_hbm, flag_ref), (node_hbm, node_ref), (bins_hbm, bins_ref),
            (logits_hbm, logits_ref), (labels_hbm, labels_ref),
            (pg_hbm, pg_ref), (ph_hbm, ph_ref)))
    ]
    for c in loads:
        c.start()

    barrier = pltpu.get_barrier_semaphore()
    for k in range(1, n_cls):
        pl.semaphore_signal(barrier, inc=1, device_id=at_cls(k))
    for k in far:
        pl.semaphore_signal(barrier, inc=1, device_id=at_row(k))
    for k in range(1, n_feat):
        pl.semaphore_signal(
            barrier, inc=1,
            device_id={"feat": ahead(me_f, k, n_feat), "rows": me_r, "cls": me_c})

    loads[3].wait()
    lt = logits_ref[...]
    top = jnp.max(lt, axis=0, keepdims=True)
    exps = jnp.sum(jnp.exp(lt - top), axis=0, keepdims=True)
    stats[0] = jnp.concatenate([top, exps], axis=0)
    pl.semaphore_wait(barrier, n_cls + n_row + n_feat - 3)

    def stat_copy(k):
        return pltpu.make_async_remote_copy(
            src_ref=stats.at[0], dst_ref=stats.at[k],
            send_sem=t_send.at[k], recv_sem=t_recv.at[k],
            device_id=at_cls(k))

    def bins_copy(k):
        return pltpu.make_async_remote_copy(
            src_ref=sendb.at[row_peer(k)], dst_ref=bins_in.at[k],
            send_sem=b_send.at[k], recv_sem=b_recv.at[k], device_id=at_row(k))

    def grad_copy(k):
        return pltpu.make_async_remote_copy(
            src_ref=g_in.at[0], dst_ref=g_in.at[k],
            send_sem=g_send.at[k], recv_sem=g_recv.at[k],
            device_id=at_row(k))

    for k in range(1, n_cls):
        stat_copy(k).start()
    for c in loads[:3]:
        c.wait()
    node = node_ref[...]
    slot = jnp.full(node.shape, -1.0, jnp.float32)
    for q in range(pcount):
        slot = jnp.where(node == 2 * q + flag_ref[q], float(q), slot)
    tail = jnp.concatenate([slot[:half], slot[half:]], axis=1).astype(jnp.bfloat16)
    sendb[:, :, :rows_here] = bins_ref[...].astype(jnp.float32).astype(jnp.bfloat16).reshape(
        n_row, f_own, rows_here)
    for d in range(n_row):
        sendb[d, :, rows_here:] = tail
    for k in near:
        bins_copy(k).start()
    bins_in[0] = sendb[me_r]
    iota = lax.broadcasted_iota(jnp.int32, (rows_here, levels), 1).astype(jnp.bfloat16)
    own_rows = jnp.transpose(
        bins_in[0, :, :rows_here].astype(jnp.float32)).astype(jnp.bfloat16)
    for f in range(f_own):
        own_hot[f] = jnp.where(
            jnp.broadcast_to(own_rows[:, f:f + 1], (rows_here, levels)) == iota,
            jnp.bfloat16(1), jnp.bfloat16(0))
    loads[4].wait()
    for k in range(1, n_cls):
        stat_copy(k).wait_recv()
    heads = [stats[d, 0:1, :] for d in range(n_cls)]
    peak = functools.reduce(jnp.maximum, heads)
    denom = functools.reduce(
        jnp.add, [stats[d, 1:2, :] * jnp.exp(heads[d] - peak) for d in range(n_cls)])
    likely = jnp.exp(lt - peak) / denom
    classes = me_c * c_dev + lax.broadcasted_iota(jnp.int32, lt.shape, 0)
    target = (labels_ref[...] == classes).astype(jnp.float32)
    both = jnp.concatenate([likely - target, likely * (1.0 - likely)], axis=0)
    g_in[0] = both.astype(jnp.bfloat16)
    for k in near[:2]:
        grad_copy(k).start()


    def columns(k):
        g = g_in[k].astype(jnp.float32)
        tail = bins_in[k, :, rows_here:].astype(jnp.float32)
        slot = jnp.concatenate([
            jnp.broadcast_to(tail[i:i + 1, h * 128:(h + 1) * 128], (kc, 128))
            for h in range(2) for i in range(half)
        ], axis=1)
        return jnp.concatenate(
            [jnp.where(slot == float(q), g, 0.0) for q in range(pcount)], axis=0
        ).astype(jnp.bfloat16)

    def operands(group, turn):
        for k in group:
            bins_copy(k).wait_recv()
            grad_copy(k).wait_recv()
        by_row = []
        for k in group:
            bins_here = bins_in[k, :, :rows_here].astype(jnp.float32)
            if turn is not None:
                bins_here = pltpu.roll(bins_here, turn, 0)
            by_row.append(jnp.transpose(bins_here).astype(jnp.bfloat16))
        return jnp.concatenate([columns(k) for k in group], axis=1), by_row

    def tally(cols, by_row, f):
        onehot = jnp.concatenate([
            jnp.where(
                jnp.broadcast_to(b[:, f:f + 1], (rows_here, levels)) == iota,
                jnp.bfloat16(1), jnp.bfloat16(0))
            for b in by_row
        ], axis=0)
        return lax.dot_general(cols, onehot, NN, preferred_element_type=jnp.float32)

    cols = columns(0)
    for f in range(f_own):
        acc[f] = lax.dot_general(cols, own_hot[f], NN, preferred_element_type=jnp.float32)
        for k in near[2:4] if f == 2 else near[4:] if f == f_own - 1 else []:
            grad_copy(k).start()
    for group in (near[:2], near[2:4]):
        cols, by_row = operands(group, None)
        for f in range(f_own):
            acc[f] += tally(cols, by_row, f)

    for c in loads[5:]:
        c.wait()
    upper = (
        lax.broadcasted_iota(jnp.int32, (levels, levels), 0)
        <= lax.broadcasted_iota(jnp.int32, (levels, levels), 1)
    ).astype(jnp.bfloat16)
    col = lax.broadcasted_iota(jnp.int32, (nodes, 4 * pcount * c_dev), 1)
    row = lax.broadcasted_iota(jnp.int32, (nodes, 4 * pcount * c_dev), 0)
    over_classes = (
        lax.rem(col, pcount * kc) // c_dev == 2 * lax.rem(row, pcount) + row // pcount
    ).astype(jnp.bfloat16)
    parent_row = lax.broadcasted_iota(jnp.int32, (pcount, levels), 0)
    flags = jnp.zeros((pcount, levels), jnp.int32)
    for q in range(pcount):
        flags = jnp.where(parent_row == q, flag_ref[q], flags)

    def two_parts(x):
        hi = x.astype(jnp.bfloat16)
        low = (x - hi.astype(jnp.float32)).astype(jnp.bfloat16)
        return jnp.concatenate([hi, low], axis=0)

    def part_copy(j):
        owner = ahead(me_c, j, n_cls)
        return pltpu.make_async_remote_copy(
            src_ref=part.at[owner], dst_ref=inbox.at[j],
            send_sem=r_send.at[j], recv_sem=r_recv.at[j],
            device_id={"cls": owner, "rows": me_r, "feat": me_f})

    def scores(counts, f):
        small = counts.reshape(pcount, kc, levels)
        small_g, small_h = small[:, :c_dev], small[:, c_dev:]
        sib_g, sib_h = pg_ref[:, f] - small_g, ph_ref[:, f] - small_h
        flat = jnp.concatenate([
            jnp.concatenate([small_g, sib_g], axis=1).reshape(pcount * kc, levels),
            jnp.concatenate([small_h, sib_h], axis=1).reshape(pcount * kc, levels),
        ], axis=0)
        size = flat.shape[0]
        left = lax.dot_general(two_parts(flat), upper, NN, preferred_element_type=jnp.float32)
        left = left[:size] + left[size:]
        lg, lh = left[:size // 2], left[size // 2:]
        wg, wh = lg[:, levels - 1:], lh[:, levels - 1:]
        term = leaf_term(lg, lh) + leaf_term(wg - lg, wh - lh) - leaf_term(wg, wh)
        sums = lax.dot_general(
            over_classes, two_parts(term), NN, preferred_element_type=jnp.float32)
        small_s, sib_s = sums[:pcount], sums[pcount:]
        part[f, :pcount] = jnp.where(flags == 0, small_s, sib_s)
        part[f, pcount:] = jnp.where(flags == 0, sib_s, small_s)

    first_f = ahead(me_c, 1, n_cls)
    cols, by_row = operands(near[4:], ahead(0, f_own - first_f, f_own))
    def place(j):
        return ahead(first_f, j - 1, f_own)

    counts = acc[place(1)] + tally(cols, by_row, 0)
    for j in range(1, n_cls + 1):
        f, ready = place(j), counts
        if j < n_cls:
            counts = acc[place(j + 1)] + tally(cols, by_row, j)
        scores(ready, f)
        acc[f] = ready
        if j < n_cls:
            part_copy(j).start()

    def small_and_sibling(q):
        small = acc[:, pl.ds(pl.multiple_of(q * kc, kc), kc), :]
        small_g, small_h = small[:, :c_dev], small[:, c_dev:]
        return small_g, small_h, pg_ref[q] - small_g, ph_ref[q] - small_h

    mine = part[me_c]
    for j in range(1, n_cls):
        part_copy(j).wait_recv()
        mine = mine + inbox[j]
    mine = mine * (1.0 / (c_dev * n_cls))
    full[me_c] = mine

    def full_copy(k):
        return pltpu.make_async_remote_copy(
            src_ref=full.at[me_c], dst_ref=full.at[me_c],
            send_sem=a_send.at[k], recv_sem=a_recv.at[k],
            device_id=at_cls(k))

    lanes = levels // 2
    node_row = lax.broadcasted_iota(jnp.int32, (nodes, lanes), 0)
    node_of_row = 2 * lax.rem(node_row, pcount) + node_row // pcount
    here = node_of_row == lax.broadcasted_iota(jnp.int32, (nodes, lanes), 1)
    over_bins = jnp.max(
        jnp.maximum(mine[:, :lanes], mine[:, lanes:]), axis=1, keepdims=True)
    tops[0] = jnp.max(
        jnp.where(here, jnp.broadcast_to(over_bins, here.shape), -jnp.inf),
        axis=0, keepdims=True)

    def top_copy(k):
        return pltpu.make_async_remote_copy(
            src_ref=tops.at[0], dst_ref=tops.at[k],
            send_sem=m_send.at[k], recv_sem=m_recv.at[k],
            device_id=grid_peer(grid_steps[k - 1]))

    def peak_copy(k):
        return pltpu.make_async_remote_copy(
            src_ref=peaks.at[0], dst_ref=peaks.at[k],
            send_sem=z_send.at[k], recv_sem=z_recv.at[k],
            device_id=wide_peer(wide_steps[k - 1]))

    n_grid, n_wide = len(grid_steps) + 1, len(wide_steps) + 1
    for k in range(1, n_grid):
        top_copy(k).start()
    for k in range(1, n_cls):
        full_copy(k).start()

    def write(q, carry):
        small_g, small_h, sib_g, sib_h = small_and_sibling(q)
        zero = flag_ref[q] == 0
        cg_ref[2 * q] = jnp.where(zero, small_g, sib_g)
        ch_ref[2 * q] = jnp.where(zero, small_h, sib_h)
        cg_ref[2 * q + 1] = jnp.where(zero, sib_g, small_g)
        ch_ref[2 * q + 1] = jnp.where(zero, sib_h, small_h)
        return carry

    lax.fori_loop(0, pcount, write, 0)
    stores = [
        pltpu.make_async_copy(cg_ref, cg_hbm, out_sem.at[0]),
        pltpu.make_async_copy(ch_ref, ch_hbm, out_sem.at[1]),
    ]
    for c in stores:
        c.start()

    for k in range(1, n_cls):
        stat_copy(k).wait_send()
        part_copy(k).wait_send()
    for k in range(1, n_row):
        bins_copy(k).wait_send()
        grad_copy(k).wait_send()
    highest = tops[0]
    for k in range(1, n_grid):
        top_copy(k).wait_recv()
        highest = jnp.maximum(highest, tops[k])
    peaks[0] = highest
    for k in range(1, n_wide):
        peak_copy(k).start()
    for k in range(1, n_grid):
        top_copy(k).wait_send()
    for k in range(1, n_cls):
        full_copy(k).wait()
    for n in range(nodes):
        at = n // 2 + (n % 2) * pcount
        gains_ref[n] = jnp.concatenate([full[f, at:at + 1] for f in range(f_own)], axis=0)
    stores.append(pltpu.make_async_copy(gains_ref, gains_hbm, out_sem.at[2]))
    stores[-1].start()
    for k in range(1, n_wide):
        peak_copy(k).wait_recv()
        highest = jnp.maximum(highest, peaks[k])
    best_ref[...] = highest[:, :nodes]

    for c in stores:
        c.wait()
    for k in range(1, n_wide):
        peak_copy(k).wait_send()


def store_kernel(cg, ch, gains, best, cg_out, ch_out, gains_out, best_out, *scratch):
    held, (in_sem, out_sem) = scratch[:4], scratch[4:]
    moves = []
    for src, via, dst in zip((cg, ch, gains, best), held, (cg_out, ch_out, gains_out, best_out)):
        pieces = 4 if src.shape[0] % 4 == 0 and len(src.shape) == 4 else 1
        size = src.shape[0] // pieces
        for p in range(pieces):
            moves.append([r.at[pl.ds(p * size, size)] for r in (src, via, dst)])
    first = [pltpu.make_async_copy(m[0], m[1], in_sem.at[i]) for i, m in enumerate(moves)]
    second = [pltpu.make_async_copy(m[1], m[2], out_sem.at[i]) for i, m in enumerate(moves)]
    for c in first:
        c.start()
    for a, b in zip(first, second):
        a.wait()
        b.start()
    for c in second:
        c.wait()


def per_device(bins, logits, labels, node_ids, small_flag, parent_grad, parent_hess):
    n_row = lax.axis_size("rows")
    n_cls = lax.axis_size("cls")
    n_grid = n_row * (lax.axis_size("feat") // 2)
    n_wide = 2 * n_cls
    rows_here, c_dev = logits.shape
    pcount, f_own, _, levels = parent_grad.shape
    nodes = 2 * pcount
    share = nodes // n_cls
    kc = 2 * c_dev
    lanes = levels // 2
    vmem = pl.BlockSpec(memory_space=pltpu.VMEM)
    hbm = pl.BlockSpec(memory_space=pltpu.HBM)
    dma = pltpu.SemaphoreType.DMA
    f32, bf16 = jnp.float32, jnp.bfloat16

    child_grad, child_hess, gains, best = pl.pallas_call(
        level_kernel,
        out_shape=(
            jax.ShapeDtypeStruct((nodes, f_own, c_dev, levels), f32),
            jax.ShapeDtypeStruct((nodes, f_own, c_dev, levels), f32),
            jax.ShapeDtypeStruct((nodes, f_own, levels), f32),
            jax.ShapeDtypeStruct((1, nodes), f32),
        ),
        in_specs=[hbm] * 7,
        out_specs=(hbm, hbm, hbm, vmem),
        scratch_shapes=[
            pltpu.VMEM((nodes, f_own, c_dev, levels), f32),
            pltpu.VMEM((nodes, f_own, c_dev, levels), f32),
            pltpu.VMEM((nodes, f_own, levels), f32),
            pltpu.VMEM((f_own, nodes, levels), f32),
            dma((3,)),
            pltpu.VMEM((n_row * f_own, rows_here), jnp.int32),
            pltpu.VMEM((c_dev, rows_here), f32),
            pltpu.VMEM((1, rows_here), jnp.int32),
            pltpu.VMEM((rows_here // 128, 128), jnp.int32),
            pltpu.SMEM((pcount,), jnp.int32),
            pltpu.VMEM(parent_grad.shape, f32),
            pltpu.VMEM(parent_hess.shape, f32),
            dma((7,)),
            pltpu.VMEM((n_row, f_own, rows_here + rows_here // f_own), bf16),
            pltpu.VMEM((n_row, f_own, rows_here + rows_here // f_own), bf16),
            pltpu.VMEM((f_own, rows_here, levels), bf16),
            pltpu.VMEM((n_row, kc, rows_here), bf16),
            pltpu.VMEM((n_cls, 2, rows_here), f32),
            pltpu.VMEM((f_own, pcount * kc, levels), f32),
            pltpu.VMEM((f_own, nodes, levels), f32),
            pltpu.VMEM((n_cls, nodes, levels), f32),
            pltpu.VMEM((n_grid, 1, lanes), f32),
            pltpu.VMEM((n_wide, 1, lanes), f32),
            dma((n_row,)), dma((n_row,)),
            dma((n_cls,)), dma((n_cls,)), dma((n_row,)), dma((n_row,)),
            dma((n_cls,)), dma((n_cls,)), dma((n_cls,)), dma((n_cls,)),
            dma((n_grid,)), dma((n_grid,)), dma((n_wide,)), dma((n_wide,)),
        ],
        compiler_params=pltpu.CompilerParams(
            collective_id=0, has_side_effects=True, vmem_limit_bytes=60 << 20),
        name="level_step",
    )(
        bins.T, logits.T, labels.reshape(1, rows_here), node_ids.reshape(rows_here // 128, 128),
        small_flag, parent_grad, parent_hess,
    )
    results = (child_grad, child_hess, gains, best)
    child_grad, child_hess, gains, best = pl.pallas_call(
        store_kernel,
        out_shape=tuple(jax.ShapeDtypeStruct(r.shape, r.dtype) for r in results),
        in_specs=[hbm] * 4,
        out_specs=(hbm,) * 4,
        scratch_shapes=[pltpu.VMEM(r.shape, r.dtype) for r in results] + [dma((10,)), dma((10,))],
        compiler_params=pltpu.CompilerParams(vmem_limit_bytes=60 << 20),
        name="store_results",
    )(*results)
    return child_grad, child_hess, gains, best.reshape(nodes)


def solution(mesh):
    in_specs = (
        P("rows", "feat"),
        P("rows", "cls"),
        P("rows"),
        P("rows"),
        P(),
        P(None, ("feat", "rows"), "cls", None),
        P(None, ("feat", "rows"), "cls", None),
    )
    out_specs = (
        P(None, ("feat", "rows"), "cls", None),
        P(None, ("feat", "rows"), "cls", None),
        P(None, ("feat", "rows"), None),
        P(),
    )
    return jax.shard_map(
        per_device, mesh=mesh, in_specs=in_specs, out_specs=out_specs, check_vma=False
    )
```

```python
import functools

import jax
import jax.numpy as jnp
from jax import lax
from jax.experimental import pallas as pl
from jax.experimental.pallas import tpu as pltpu
from jax.sharding import PartitionSpec as P

ridge_weight = 1.0
NN = (((1,), (0,)), ((), ()))


def leaf_term(grad_sum, hess_sum):
    return grad_sum * grad_sum / (jnp.maximum(hess_sum, 0.0) + ridge_weight)


def level_kernel(
    bins_hbm, logits_hbm, labels_hbm, node_hbm, flag_hbm, pg_hbm, ph_hbm,
    cg_hbm, ch_hbm, gains_hbm, best_ref,
    cg_ref, ch_ref, gains_ref, full, out_sem, bins_ref, logits_ref, labels_ref, node_ref, flag_ref, pg_ref, ph_ref, load_sem,
    sendb, bins_in, own_hot, g_in, stats, acc, part, inbox, tops, peaks,
    b_send, b_recv, t_send, t_recv, g_send, g_recv,
    r_send, r_recv, a_send, a_recv, m_send, m_recv, z_send, z_recv,
):
    n_row = lax.axis_size("rows")
    n_cls = lax.axis_size("cls")
    n_feat = lax.axis_size("feat")
    me_r = lax.axis_index("rows")
    me_c = lax.axis_index("cls")
    me_f = lax.axis_index("feat")
    pcount, f_own, c_dev, levels = pg_ref.shape
    rows_here = labels_ref.shape[1]
    assert f_own == n_cls
    kc = 2 * c_dev
    nodes = 2 * pcount
    share = nodes // n_cls
    n_x = n_cls // 2
    n_core = n_feat // 2
    half = rows_here // 128 // 2
    near = [k for pair in zip(range(1, n_row // 2), range(n_row - 1, n_row // 2, -1)) for k in pair]
    near = near + [n_row // 2]

    far = near[::-1]
    ring_x = [n_x // 2] + [d for i in range(1, n_x // 2) for d in (i, n_x - i)]
    cls_steps = [(1, d) for d in ring_x + [0]] + [(0, d) for d in ring_x]
    grid_steps = [(d, e) for d in far for e in range(n_core)] + [
        (0, e) for e in range(1, n_core)]
    wide_steps = [(1, c) for c in cls_steps + [(0, 0)]] + [(0, c) for c in cls_steps]

    me_x, me_y = lax.rem(me_c, n_x), me_c // n_x
    me_core, me_low = lax.rem(me_f, n_core), me_f // n_core

    def ahead(place, step, size):
        moved = place + step
        return jnp.where(moved >= size, moved - size, moved)

    def row_peer(k):
        return ahead(me_r, k, n_row)

    def cls_peer(step):
        dy, dx = step
        return ahead(me_y, dy, 2) * n_x + ahead(me_x, dx, n_x)

    def grid_peer(step):
        dr, dc = step
        return {
            "cls": me_c, "rows": row_peer(dr),
            "feat": me_low * n_core + ahead(me_core, dc, n_core)}

    def wide_peer(step):
        dl, c = step
        return {
            "cls": cls_peer(c), "rows": me_r,
            "feat": ahead(me_low, dl, 2) * n_core + me_core}

    def at_row(k):
        return {"rows": row_peer(k), "feat": me_f, "cls": me_c}

    def at_cls(k):
        return {"cls": cls_peer(cls_steps[k - 1]), "rows": me_r, "feat": me_f}

    loads = [
        pltpu.make_async_copy(src, dst, load_sem.at[i])
        for i, (src, dst) in enumerate((
            (flag_hbm, flag_ref), (node_hbm, node_ref), (bins_hbm, bins_ref),
            (logits_hbm, logits_ref), (labels_hbm, labels_ref),
            (pg_hbm, pg_ref), (ph_hbm, ph_ref)))
    ]
    for c in loads:
        c.start()

    barrier = pltpu.get_barrier_semaphore()
    for k in range(1, n_cls):
        pl.semaphore_signal(barrier, inc=1, device_id=at_cls(k))
    for k in far:
        pl.semaphore_signal(barrier, inc=1, device_id=at_row(k))
    for k in range(1, n_feat):
        pl.semaphore_signal(
            barrier, inc=1,
            device_id={"feat": ahead(me_f, k, n_feat), "rows": me_r, "cls": me_c})

    loads[3].wait()
    lt = logits_ref[...]
    top = jnp.max(lt, axis=0, keepdims=True)
    exps = jnp.sum(jnp.exp(lt - top), axis=0, keepdims=True)
    stats[0] = jnp.concatenate([top, exps], axis=0)
    pl.semaphore_wait(barrier, n_cls + n_row + n_feat - 3)

    def stat_copy(k):
        return pltpu.make_async_remote_copy(
            src_ref=stats.at[0], dst_ref=stats.at[k],
            send_sem=t_send.at[k], recv_sem=t_recv.at[k],
            device_id=at_cls(k))

    def bins_copy(k):
        return pltpu.make_async_remote_copy(
            src_ref=sendb.at[row_peer(k)], dst_ref=bins_in.at[k],
            send_sem=b_send.at[k], recv_sem=b_recv.at[k], device_id=at_row(k))

    def grad_copy(k):
        return pltpu.make_async_remote_copy(
            src_ref=g_in.at[0], dst_ref=g_in.at[k],
            send_sem=g_send.at[k], recv_sem=g_recv.at[k],
            device_id=at_row(k))

    for k in range(1, n_cls):
        stat_copy(k).start()
    for c in loads[:3]:
        c.wait()
    node = node_ref[...]
    slot = jnp.full(node.shape, -1.0, jnp.float32)
    for q in range(pcount):
        slot = jnp.where(node == 2 * q + flag_ref[q], float(q), slot)
    tail = jnp.concatenate([slot[:half], slot[half:]], axis=1).astype(jnp.bfloat16)
    sendb[:, :, :rows_here] = bins_ref[...].astype(jnp.float32).astype(jnp.bfloat16).reshape(
        n_row, f_own, rows_here)
    for d in range(n_row):
        sendb[d, :, rows_here:] = tail
    for k in near:
        bins_copy(k).start()
    bins_in[0] = sendb[me_r]
    iota = lax.broadcasted_iota(jnp.int32, (rows_here, levels), 1).astype(jnp.bfloat16)
    own_rows = jnp.transpose(
        bins_in[0, :, :rows_here].astype(jnp.float32)).astype(jnp.bfloat16)
    for f in range(f_own):
        own_hot[f] = jnp.where(
            jnp.broadcast_to(own_rows[:, f:f + 1], (rows_here, levels)) == iota,
            jnp.bfloat16(1), jnp.bfloat16(0))
    loads[4].wait()
    for k in range(1, n_cls):
        stat_copy(k).wait_recv()
    heads = [stats[d, 0:1, :] for d in range(n_cls)]
    peak = functools.reduce(jnp.maximum, heads)
    denom = functools.reduce(
        jnp.add, [stats[d, 1:2, :] * jnp.exp(heads[d] - peak) for d in range(n_cls)])
    likely = jnp.exp(lt - peak) / denom
    classes = me_c * c_dev + lax.broadcasted_iota(jnp.int32, lt.shape, 0)
    target = (labels_ref[...] == classes).astype(jnp.float32)
    both = jnp.concatenate([likely - target, likely * (1.0 - likely)], axis=0)
    g_in[0] = both.astype(jnp.bfloat16)
    for k in near[:2]:
        grad_copy(k).start()


    def columns(k):
        g = g_in[k].astype(jnp.float32)
        tail = bins_in[k, :, rows_here:].astype(jnp.float32)
        slot = jnp.concatenate([
            jnp.broadcast_to(tail[i:i + 1, h * 128:(h + 1) * 128], (kc, 128))
            for h in range(2) for i in range(half)
        ], axis=1)
        return jnp.concatenate(
            [jnp.where(slot == float(q), g, 0.0) for q in range(pcount)], axis=0
        ).astype(jnp.bfloat16)

    def operands(group, turn):
        for k in group:
            bins_copy(k).wait_recv()
            grad_copy(k).wait_recv()
        by_row = []
        for k in group:
            bins_here = bins_in[k, :, :rows_here].astype(jnp.float32)
            if turn is not None:
                bins_here = pltpu.roll(bins_here, turn, 0)
            by_row.append(jnp.transpose(bins_here).astype(jnp.bfloat16))
        return jnp.concatenate([columns(k) for k in group], axis=1), by_row

    def tally(cols, by_row, f):
        onehot = jnp.concatenate([
            jnp.where(
                jnp.broadcast_to(b[:, f:f + 1], (rows_here, levels)) == iota,
                jnp.bfloat16(1), jnp.bfloat16(0))
            for b in by_row
        ], axis=0)
        return lax.dot_general(cols, onehot, NN, preferred_element_type=jnp.float32)

    cols = columns(0)
    for f in range(f_own):
        acc[f] = lax.dot_general(cols, own_hot[f], NN, preferred_element_type=jnp.float32)
        for k in near[2:4] if f == 2 else near[4:] if f == f_own - 1 else []:
            grad_copy(k).start()
    for group in (near[:2], near[2:4]):
        cols, by_row = operands(group, None)
        for f in range(f_own):
            acc[f] += tally(cols, by_row, f)

    for c in loads[5:]:
        c.wait()
    upper = (
        lax.broadcasted_iota(jnp.int32, (levels, levels), 0)
        <= lax.broadcasted_iota(jnp.int32, (levels, levels), 1)
    ).astype(jnp.bfloat16)
    col = lax.broadcasted_iota(jnp.int32, (nodes, 4 * pcount * c_dev), 1)
    row = lax.broadcasted_iota(jnp.int32, (nodes, 4 * pcount * c_dev), 0)
    over_classes = (
        lax.rem(col, pcount * kc) // c_dev == 2 * lax.rem(row, pcount) + row // pcount
    ).astype(jnp.bfloat16)
    parent_row = lax.broadcasted_iota(jnp.int32, (pcount, levels), 0)
    flags = jnp.zeros((pcount, levels), jnp.int32)
    for q in range(pcount):
        flags = jnp.where(parent_row == q, flag_ref[q], flags)

    def two_parts(x):
        hi = x.astype(jnp.bfloat16)
        low = (x - hi.astype(jnp.float32)).astype(jnp.bfloat16)
        return jnp.concatenate([hi, low], axis=0)

    def part_copy(j):
        owner = ahead(me_c, j, n_cls)
        return pltpu.make_async_remote_copy(
            src_ref=part.at[owner], dst_ref=inbox.at[j],
            send_sem=r_send.at[j], recv_sem=r_recv.at[j],
            device_id={"cls": owner, "rows": me_r, "feat": me_f})

    def scores(counts, f):
        small = counts.reshape(pcount, kc, levels)
        small_g, small_h = small[:, :c_dev], small[:, c_dev:]
        sib_g, sib_h = pg_ref[:, f] - small_g, ph_ref[:, f] - small_h
        flat = jnp.concatenate([
            jnp.concatenate([small_g, sib_g], axis=1).reshape(pcount * kc, levels),
            jnp.concatenate([small_h, sib_h], axis=1).reshape(pcount * kc, levels),
        ], axis=0)
        size = flat.shape[0]
        left = lax.dot_general(two_parts(flat), upper, NN, preferred_element_type=jnp.float32)
        left = left[:size] + left[size:]
        lg, lh = left[:size // 2], left[size // 2:]
        wg, wh = lg[:, levels - 1:], lh[:, levels - 1:]
        term = leaf_term(lg, lh) + leaf_term(wg - lg, wh - lh) - leaf_term(wg, wh)
        sums = lax.dot_general(
            over_classes, two_parts(term), NN, preferred_element_type=jnp.float32)
        small_s, sib_s = sums[:pcount], sums[pcount:]
        part[f, :pcount] = jnp.where(flags == 0, small_s, sib_s)
        part[f, pcount:] = jnp.where(flags == 0, sib_s, small_s)

    first_f = ahead(me_c, 1, n_cls)
    cols, by_row = operands(near[4:], ahead(0, f_own - first_f, f_own))
    def place(j):
        return ahead(first_f, j - 1, f_own)

    counts = acc[place(1)] + tally(cols, by_row, 0)
    for j in range(1, n_cls + 1):
        f, ready = place(j), counts
        if j < n_cls:
            counts = acc[place(j + 1)] + tally(cols, by_row, j)
        scores(ready, f)
        acc[f] = ready
        if j < n_cls:
            part_copy(j).start()

    def small_and_sibling(q):
        small = acc[:, pl.ds(pl.multiple_of(q * kc, kc), kc), :]
        small_g, small_h = small[:, :c_dev], small[:, c_dev:]
        return small_g, small_h, pg_ref[q] - small_g, ph_ref[q] - small_h

    mine = part[me_c]
    for j in range(1, n_cls):
        part_copy(j).wait_recv()
        mine = mine + inbox[j]
    mine = mine * (1.0 / (c_dev * n_cls))
    full[me_c] = mine

    def full_copy(k):
        return pltpu.make_async_remote_copy(
            src_ref=full.at[me_c], dst_ref=full.at[me_c],
            send_sem=a_send.at[k], recv_sem=a_recv.at[k],
            device_id=at_cls(k))

    lanes = levels // 2
    node_row = lax.broadcasted_iota(jnp.int32, (nodes, lanes), 0)
    node_of_row = 2 * lax.rem(node_row, pcount) + node_row // pcount
    here = node_of_row == lax.broadcasted_iota(jnp.int32, (nodes, lanes), 1)
    over_bins = jnp.max(
        jnp.maximum(mine[:, :lanes], mine[:, lanes:]), axis=1, keepdims=True)
    tops[0] = jnp.max(
        jnp.where(here, jnp.broadcast_to(over_bins, here.shape), -jnp.inf),
        axis=0, keepdims=True)

    def top_copy(k):
        return pltpu.make_async_remote_copy(
            src_ref=tops.at[0], dst_ref=tops.at[k],
            send_sem=m_send.at[k], recv_sem=m_recv.at[k],
            device_id=grid_peer(grid_steps[k - 1]))

    def peak_copy(k):
        return pltpu.make_async_remote_copy(
            src_ref=peaks.at[0], dst_ref=peaks.at[k],
            send_sem=z_send.at[k], recv_sem=z_recv.at[k],
            device_id=wide_peer(wide_steps[k - 1]))

    n_grid, n_wide = len(grid_steps) + 1, len(wide_steps) + 1
    for k in range(1, n_grid):
        top_copy(k).start()
    for k in range(1, n_cls):
        full_copy(k).start()

    def write(q, carry):
        small_g, small_h, sib_g, sib_h = small_and_sibling(q)
        zero = flag_ref[q] == 0
        cg_ref[2 * q] = jnp.where(zero, small_g, sib_g)
        ch_ref[2 * q] = jnp.where(zero, small_h, sib_h)
        cg_ref[2 * q + 1] = jnp.where(zero, sib_g, small_g)
        ch_ref[2 * q + 1] = jnp.where(zero, sib_h, small_h)
        return carry

    lax.fori_loop(0, pcount // 2, write, 0)
    for k in range(1, n_cls):
        stat_copy(k).wait_send()
        part_copy(k).wait_send()
    for k in range(1, n_row):
        bins_copy(k).wait_send()
        grad_copy(k).wait_send()
    highest = tops[0]
    for k in range(1, n_grid):
        top_copy(k).wait_recv()
        highest = jnp.maximum(highest, tops[k])
    peaks[0] = highest
    for k in range(1, n_wide):
        peak_copy(k).start()
    lax.fori_loop(pcount // 2, pcount, write, 0)
    stores = [
        pltpu.make_async_copy(cg_ref, cg_hbm, out_sem.at[0]),
        pltpu.make_async_copy(ch_ref, ch_hbm, out_sem.at[1]),
    ]
    for c in stores:
        c.start()

    for k in range(1, n_grid):
        top_copy(k).wait_send()
    for k in range(1, n_cls):
        full_copy(k).wait()
    for n in range(nodes):
        at = n // 2 + (n % 2) * pcount
        gains_ref[n] = jnp.concatenate([full[f, at:at + 1] for f in range(f_own)], axis=0)
    stores.append(pltpu.make_async_copy(gains_ref, gains_hbm, out_sem.at[2]))
    stores[-1].start()
    for k in range(1, n_wide):
        peak_copy(k).wait_recv()
        highest = jnp.maximum(highest, peaks[k])
    best_ref[...] = highest[:, :nodes]

    for c in stores:
        c.wait()
    for k in range(1, n_wide):
        peak_copy(k).wait_send()


def store_kernel(cg, ch, gains, best, cg_out, ch_out, gains_out, best_out, *scratch):
    held, (in_sem, out_sem) = scratch[:4], scratch[4:]
    moves = []
    for src, via, dst in zip((cg, ch, gains, best), held, (cg_out, ch_out, gains_out, best_out)):
        pieces = 4 if src.shape[0] % 4 == 0 and len(src.shape) == 4 else 1
        size = src.shape[0] // pieces
        for p in range(pieces):
            moves.append([r.at[pl.ds(p * size, size)] for r in (src, via, dst)])
    first = [pltpu.make_async_copy(m[0], m[1], in_sem.at[i]) for i, m in enumerate(moves)]
    second = [pltpu.make_async_copy(m[1], m[2], out_sem.at[i]) for i, m in enumerate(moves)]
    for c in first:
        c.start()
    for a, b in zip(first, second):
        a.wait()
        b.start()
    for c in second:
        c.wait()


def per_device(bins, logits, labels, node_ids, small_flag, parent_grad, parent_hess):
    n_row = lax.axis_size("rows")
    n_cls = lax.axis_size("cls")
    n_grid = n_row * (lax.axis_size("feat") // 2)
    n_wide = 2 * n_cls
    rows_here, c_dev = logits.shape
    pcount, f_own, _, levels = parent_grad.shape
    nodes = 2 * pcount
    share = nodes // n_cls
    kc = 2 * c_dev
    lanes = levels // 2
    vmem = pl.BlockSpec(memory_space=pltpu.VMEM)
    hbm = pl.BlockSpec(memory_space=pltpu.HBM)
    dma = pltpu.SemaphoreType.DMA
    f32, bf16 = jnp.float32, jnp.bfloat16

    child_grad, child_hess, gains, best = pl.pallas_call(
        level_kernel,
        out_shape=(
            jax.ShapeDtypeStruct((nodes, f_own, c_dev, levels), f32),
            jax.ShapeDtypeStruct((nodes, f_own, c_dev, levels), f32),
            jax.ShapeDtypeStruct((nodes, f_own, levels), f32),
            jax.ShapeDtypeStruct((1, nodes), f32),
        ),
        in_specs=[hbm] * 7,
        out_specs=(hbm, hbm, hbm, vmem),
        scratch_shapes=[
            pltpu.VMEM((nodes, f_own, c_dev, levels), f32),
            pltpu.VMEM((nodes, f_own, c_dev, levels), f32),
            pltpu.VMEM((nodes, f_own, levels), f32),
            pltpu.VMEM((f_own, nodes, levels), f32),
            dma((3,)),
            pltpu.VMEM((n_row * f_own, rows_here), jnp.int32),
            pltpu.VMEM((c_dev, rows_here), f32),
            pltpu.VMEM((1, rows_here), jnp.int32),
            pltpu.VMEM((rows_here // 128, 128), jnp.int32),
            pltpu.SMEM((pcount,), jnp.int32),
            pltpu.VMEM(parent_grad.shape, f32),
            pltpu.VMEM(parent_hess.shape, f32),
            dma((7,)),
            pltpu.VMEM((n_row, f_own, rows_here + rows_here // f_own), bf16),
            pltpu.VMEM((n_row, f_own, rows_here + rows_here // f_own), bf16),
            pltpu.VMEM((f_own, rows_here, levels), bf16),
            pltpu.VMEM((n_row, kc, rows_here), bf16),
            pltpu.VMEM((n_cls, 2, rows_here), f32),
            pltpu.VMEM((f_own, pcount * kc, levels), f32),
            pltpu.VMEM((f_own, nodes, levels), f32),
            pltpu.VMEM((n_cls, nodes, levels), f32),
            pltpu.VMEM((n_grid, 1, lanes), f32),
            pltpu.VMEM((n_wide, 1, lanes), f32),
            dma((n_row,)), dma((n_row,)),
            dma((n_cls,)), dma((n_cls,)), dma((n_row,)), dma((n_row,)),
            dma((n_cls,)), dma((n_cls,)), dma((n_cls,)), dma((n_cls,)),
            dma((n_grid,)), dma((n_grid,)), dma((n_wide,)), dma((n_wide,)),
        ],
        compiler_params=pltpu.CompilerParams(
            collective_id=0, has_side_effects=True, vmem_limit_bytes=60 << 20),
        name="level_step",
    )(
        bins.T, logits.T, labels.reshape(1, rows_here), node_ids.reshape(rows_here // 128, 128),
        small_flag, parent_grad, parent_hess,
    )
    results = (child_grad, child_hess, gains, best)
    child_grad, child_hess, gains, best = pl.pallas_call(
        store_kernel,
        out_shape=tuple(jax.ShapeDtypeStruct(r.shape, r.dtype) for r in results),
        in_specs=[hbm] * 4,
        out_specs=(hbm,) * 4,
        scratch_shapes=[pltpu.VMEM(r.shape, r.dtype) for r in results] + [dma((10,)), dma((10,))],
        compiler_params=pltpu.CompilerParams(vmem_limit_bytes=60 << 20),
        name="store_results",
    )(*results)
    return child_grad, child_hess, gains, best.reshape(nodes)


def solution(mesh):
    in_specs = (
        P("rows", "feat"),
        P("rows", "cls"),
        P("rows"),
        P("rows"),
        P(),
        P(None, ("feat", "rows"), "cls", None),
        P(None, ("feat", "rows"), "cls", None),
    )
    out_specs = (
        P(None, ("feat", "rows"), "cls", None),
        P(None, ("feat", "rows"), "cls", None),
        P(None, ("feat", "rows"), None),
        P(),
    )
    return jax.shard_map(
        per_device, mesh=mesh, in_specs=in_specs, out_specs=out_specs, check_vma=False
    )
```

```python
import functools

import jax
import jax.numpy as jnp
from jax import lax
from jax.experimental import pallas as pl
from jax.experimental.pallas import tpu as pltpu
from jax.sharding import PartitionSpec as P

ridge_weight = 1.0
NN = (((1,), (0,)), ((), ()))


def leaf_term(grad_sum, hess_sum):
    return grad_sum * grad_sum / (jnp.maximum(hess_sum, 0.0) + ridge_weight)


def level_kernel(
    bins_hbm, logits_hbm, labels_hbm, node_hbm, flag_hbm, pg_hbm, ph_hbm,
    cg_hbm, ch_hbm, gains_hbm, best_ref,
    cg_ref, ch_ref, gains_ref, full, out_sem, bins_ref, logits_ref, labels_ref, node_ref, flag_ref, pg_ref, ph_ref, load_sem,
    sendb, bins_in, own_hot, g_in, stats, acc, part, inbox, tops, peaks,
    b_send, b_recv, t_send, t_recv, g_send, g_recv,
    r_send, r_recv, a_send, a_recv, m_send, m_recv, z_send, z_recv,
):
    n_row = lax.axis_size("rows")
    n_cls = lax.axis_size("cls")
    n_feat = lax.axis_size("feat")
    me_r = lax.axis_index("rows")
    me_c = lax.axis_index("cls")
    me_f = lax.axis_index("feat")
    pcount, f_own, c_dev, levels = pg_ref.shape
    rows_here = labels_ref.shape[1]
    assert f_own == n_cls
    kc = 2 * c_dev
    nodes = 2 * pcount
    share = nodes // n_cls
    n_x = n_cls // 2
    n_core = n_feat // 2
    half = rows_here // 128 // 2
    near = [k for pair in zip(range(1, n_row // 2), range(n_row - 1, n_row // 2, -1)) for k in pair]
    near = near + [n_row // 2]

    far = near[::-1]
    ring_x = [n_x // 2] + [d for i in range(1, n_x // 2) for d in (i, n_x - i)]
    cls_steps = [(1, d) for d in ring_x + [0]] + [(0, d) for d in ring_x]
    grid_steps = [(d, e) for d in far for e in range(n_core)] + [
        (0, e) for e in range(1, n_core)]
    wide_steps = [(1, c) for c in cls_steps + [(0, 0)]] + [(0, c) for c in cls_steps]

    me_x, me_y = lax.rem(me_c, n_x), me_c // n_x
    me_core, me_low = lax.rem(me_f, n_core), me_f // n_core

    def ahead(place, step, size):
        moved = place + step
        return jnp.where(moved >= size, moved - size, moved)

    def row_peer(k):
        return ahead(me_r, k, n_row)

    def cls_peer(step):
        dy, dx = step
        return ahead(me_y, dy, 2) * n_x + ahead(me_x, dx, n_x)

    def grid_peer(step):
        dr, dc = step
        return {
            "cls": me_c, "rows": row_peer(dr),
            "feat": me_low * n_core + ahead(me_core, dc, n_core)}

    def wide_peer(step):
        dl, c = step
        return {
            "cls": cls_peer(c), "rows": me_r,
            "feat": ahead(me_low, dl, 2) * n_core + me_core}

    def at_row(k):
        return {"rows": row_peer(k), "feat": me_f, "cls": me_c}

    def at_cls(k):
        return {"cls": cls_peer(cls_steps[k - 1]), "rows": me_r, "feat": me_f}

    loads = [
        pltpu.make_async_copy(src, dst, load_sem.at[i])
        for i, (src, dst) in enumerate((
            (flag_hbm, flag_ref), (node_hbm, node_ref), (bins_hbm, bins_ref),
            (logits_hbm, logits_ref), (labels_hbm, labels_ref),
            (pg_hbm, pg_ref), (ph_hbm, ph_ref)))
    ]
    for c in loads:
        c.start()

    barrier = pltpu.get_barrier_semaphore()
    for k in range(1, n_cls):
        pl.semaphore_signal(barrier, inc=1, device_id=at_cls(k))
    for k in far:
        pl.semaphore_signal(barrier, inc=1, device_id=at_row(k))
    for k in range(1, n_core):
        pl.semaphore_signal(barrier, inc=1, device_id=grid_peer((0, k)))
    pl.semaphore_signal(barrier, inc=1, device_id=wide_peer((1, (0, 0))))

    loads[3].wait()
    lt = logits_ref[...]
    top = jnp.max(lt, axis=0, keepdims=True)
    exps = jnp.sum(jnp.exp(lt - top), axis=0, keepdims=True)
    stats[0] = jnp.concatenate([top, exps], axis=0)
    pl.semaphore_wait(barrier, n_cls + n_row + n_core - 2)

    def stat_copy(k):
        return pltpu.make_async_remote_copy(
            src_ref=stats.at[0], dst_ref=stats.at[k],
            send_sem=t_send.at[k], recv_sem=t_recv.at[k],
            device_id=at_cls(k))

    def bins_copy(k):
        return pltpu.make_async_remote_copy(
            src_ref=sendb.at[row_peer(k)], dst_ref=bins_in.at[k],
            send_sem=b_send.at[k], recv_sem=b_recv.at[k], device_id=at_row(k))

    def grad_copy(k):
        return pltpu.make_async_remote_copy(
            src_ref=g_in.at[0], dst_ref=g_in.at[k],
            send_sem=g_send.at[k], recv_sem=g_recv.at[k],
            device_id=at_row(k))

    for k in range(1, n_cls):
        stat_copy(k).start()
    for c in loads[:3]:
        c.wait()
    node = node_ref[...]
    slot = jnp.full(node.shape, -1.0, jnp.float32)
    for q in range(pcount):
        slot = jnp.where(node == 2 * q + flag_ref[q], float(q), slot)
    tail = jnp.concatenate([slot[:half], slot[half:]], axis=1).astype(jnp.bfloat16)
    sendb[:, :, :rows_here] = bins_ref[...].astype(jnp.float32).astype(jnp.bfloat16).reshape(
        n_row, f_own, rows_here)
    for d in range(n_row):
        sendb[d, :, rows_here:] = tail
    for k in near:
        bins_copy(k).start()
    bins_in[0] = sendb[me_r]
    iota = lax.broadcasted_iota(jnp.int32, (rows_here, levels), 1).astype(jnp.bfloat16)
    own_rows = jnp.transpose(
        bins_in[0, :, :rows_here].astype(jnp.float32)).astype(jnp.bfloat16)
    for f in range(f_own):
        own_hot[f] = jnp.where(
            jnp.broadcast_to(own_rows[:, f:f + 1], (rows_here, levels)) == iota,
            jnp.bfloat16(1), jnp.bfloat16(0))
    loads[4].wait()
    for k in range(1, n_cls):
        stat_copy(k).wait_recv()
    heads = [stats[d, 0:1, :] for d in range(n_cls)]
    peak = functools.reduce(jnp.maximum, heads)
    denom = functools.reduce(
        jnp.add, [stats[d, 1:2, :] * jnp.exp(heads[d] - peak) for d in range(n_cls)])
    likely = jnp.exp(lt - peak) / denom
    classes = me_c * c_dev + lax.broadcasted_iota(jnp.int32, lt.shape, 0)
    target = (labels_ref[...] == classes).astype(jnp.float32)
    both = jnp.concatenate([likely - target, likely * (1.0 - likely)], axis=0)
    g_in[0] = both.astype(jnp.bfloat16)
    for k in near[:2]:
        grad_copy(k).start()


    def columns(k):
        g = g_in[k].astype(jnp.float32)
        tail = bins_in[k, :, rows_here:].astype(jnp.float32)
        slot = jnp.concatenate([
            jnp.broadcast_to(tail[i:i + 1, h * 128:(h + 1) * 128], (kc, 128))
            for h in range(2) for i in range(half)
        ], axis=1)
        return jnp.concatenate(
            [jnp.where(slot == float(q), g, 0.0) for q in range(pcount)], axis=0
        ).astype(jnp.bfloat16)

    def operands(group, turn):
        for k in group:
            bins_copy(k).wait_recv()
            grad_copy(k).wait_recv()
        by_row = []
        for k in group:
            bins_here = bins_in[k, :, :rows_here].astype(jnp.float32)
            if turn is not None:
                bins_here = pltpu.roll(bins_here, turn, 0)
            by_row.append(jnp.transpose(bins_here).astype(jnp.bfloat16))
        return jnp.concatenate([columns(k) for k in group], axis=1), by_row

    def tally(cols, by_row, f):
        onehot = jnp.concatenate([
            jnp.where(
                jnp.broadcast_to(b[:, f:f + 1], (rows_here, levels)) == iota,
                jnp.bfloat16(1), jnp.bfloat16(0))
            for b in by_row
        ], axis=0)
        return lax.dot_general(cols, onehot, NN, preferred_element_type=jnp.float32)

    cols = columns(0)
    for f in range(f_own):
        acc[f] = lax.dot_general(cols, own_hot[f], NN, preferred_element_type=jnp.float32)
        for k in near[2:4] if f == 2 else near[4:] if f == f_own - 1 else []:
            grad_copy(k).start()
    for group in (near[:2], near[2:4]):
        cols, by_row = operands(group, None)
        for f in range(f_own):
            acc[f] += tally(cols, by_row, f)

    for c in loads[5:]:
        c.wait()
    upper = (
        lax.broadcasted_iota(jnp.int32, (levels, levels), 0)
        <= lax.broadcasted_iota(jnp.int32, (levels, levels), 1)
    ).astype(jnp.bfloat16)
    col = lax.broadcasted_iota(jnp.int32, (nodes, 4 * pcount * c_dev), 1)
    row = lax.broadcasted_iota(jnp.int32, (nodes, 4 * pcount * c_dev), 0)
    over_classes = (
        lax.rem(col, pcount * kc) // c_dev == 2 * lax.rem(row, pcount) + row // pcount
    ).astype(jnp.bfloat16)
    parent_row = lax.broadcasted_iota(jnp.int32, (pcount, levels), 0)
    flags = jnp.zeros((pcount, levels), jnp.int32)
    for q in range(pcount):
        flags = jnp.where(parent_row == q, flag_ref[q], flags)

    def two_parts(x):
        hi = x.astype(jnp.bfloat16)
        low = (x - hi.astype(jnp.float32)).astype(jnp.bfloat16)
        return jnp.concatenate([hi, low], axis=0)

    def part_copy(j):
        owner = ahead(me_c, j, n_cls)
        return pltpu.make_async_remote_copy(
            src_ref=part.at[owner], dst_ref=inbox.at[j],
            send_sem=r_send.at[j], recv_sem=r_recv.at[j],
            device_id={"cls": owner, "rows": me_r, "feat": me_f})

    def scores(counts, f):
        small = counts.reshape(pcount, kc, levels)
        small_g, small_h = small[:, :c_dev], small[:, c_dev:]
        sib_g, sib_h = pg_ref[:, f] - small_g, ph_ref[:, f] - small_h
        flat = jnp.concatenate([
            jnp.concatenate([small_g, sib_g], axis=1).reshape(pcount * kc, levels),
            jnp.concatenate([small_h, sib_h], axis=1).reshape(pcount * kc, levels),
        ], axis=0)
        size = flat.shape[0]
        left = lax.dot_general(two_parts(flat), upper, NN, preferred_element_type=jnp.float32)
        left = left[:size] + left[size:]
        lg, lh = left[:size // 2], left[size // 2:]
        wg, wh = lg[:, levels - 1:], lh[:, levels - 1:]
        term = leaf_term(lg, lh) + leaf_term(wg - lg, wh - lh) - leaf_term(wg, wh)
        sums = lax.dot_general(
            over_classes, two_parts(term), NN, preferred_element_type=jnp.float32)
        small_s, sib_s = sums[:pcount], sums[pcount:]
        part[f, :pcount] = jnp.where(flags == 0, small_s, sib_s)
        part[f, pcount:] = jnp.where(flags == 0, sib_s, small_s)

    first_f = ahead(me_c, 1, n_cls)
    cols, by_row = operands(near[4:], ahead(0, f_own - first_f, f_own))
    def place(j):
        return ahead(first_f, j - 1, f_own)

    counts = acc[place(1)] + tally(cols, by_row, 0)
    for j in range(1, n_cls + 1):
        f, ready = place(j), counts
        if j < n_cls:
            counts = acc[place(j + 1)] + tally(cols, by_row, j)
        scores(ready, f)
        acc[f] = ready
        if j < n_cls:
            part_copy(j).start()

    def small_and_sibling(q):
        small = acc[:, pl.ds(pl.multiple_of(q * kc, kc), kc), :]
        small_g, small_h = small[:, :c_dev], small[:, c_dev:]
        return small_g, small_h, pg_ref[q] - small_g, ph_ref[q] - small_h

    mine = part[me_c]
    for j in range(1, n_cls):
        part_copy(j).wait_recv()
        mine = mine + inbox[j]
    mine = mine * (1.0 / (c_dev * n_cls))
    full[me_c] = mine

    def full_copy(k):
        return pltpu.make_async_remote_copy(
            src_ref=full.at[me_c], dst_ref=full.at[me_c],
            send_sem=a_send.at[k], recv_sem=a_recv.at[k],
            device_id=at_cls(k))

    lanes = levels // 2
    node_row = lax.broadcasted_iota(jnp.int32, (nodes, lanes), 0)
    node_of_row = 2 * lax.rem(node_row, pcount) + node_row // pcount
    here = node_of_row == lax.broadcasted_iota(jnp.int32, (nodes, lanes), 1)
    over_bins = jnp.max(
        jnp.maximum(mine[:, :lanes], mine[:, lanes:]), axis=1, keepdims=True)
    tops[0] = jnp.max(
        jnp.where(here, jnp.broadcast_to(over_bins, here.shape), -jnp.inf),
        axis=0, keepdims=True)

    def top_copy(k):
        return pltpu.make_async_remote_copy(
            src_ref=tops.at[0], dst_ref=tops.at[k],
            send_sem=m_send.at[k], recv_sem=m_recv.at[k],
            device_id=grid_peer(grid_steps[k - 1]))

    def peak_copy(k):
        return pltpu.make_async_remote_copy(
            src_ref=peaks.at[0], dst_ref=peaks.at[k],
            send_sem=z_send.at[k], recv_sem=z_recv.at[k],
            device_id=wide_peer(wide_steps[k - 1]))

    n_grid, n_wide = len(grid_steps) + 1, len(wide_steps) + 1
    for k in range(1, n_grid):
        top_copy(k).start()
    for k in range(1, n_cls):
        full_copy(k).start()

    def write(q, carry):
        small_g, small_h, sib_g, sib_h = small_and_sibling(q)
        zero = flag_ref[q] == 0
        cg_ref[2 * q] = jnp.where(zero, small_g, sib_g)
        ch_ref[2 * q] = jnp.where(zero, small_h, sib_h)
        cg_ref[2 * q + 1] = jnp.where(zero, sib_g, small_g)
        ch_ref[2 * q + 1] = jnp.where(zero, sib_h, small_h)
        return carry

    lax.fori_loop(0, pcount // 2, write, 0)
    for k in range(1, n_cls):
        stat_copy(k).wait_send()
        part_copy(k).wait_send()
    for k in range(1, n_row):
        bins_copy(k).wait_send()
        grad_copy(k).wait_send()
    highest = tops[0]
    for k in range(1, n_grid):
        top_copy(k).wait_recv()
        highest = jnp.maximum(highest, tops[k])
    peaks[0] = highest
    for k in range(1, n_wide):
        peak_copy(k).start()
    lax.fori_loop(pcount // 2, pcount, write, 0)
    stores = [
        pltpu.make_async_copy(cg_ref, cg_hbm, out_sem.at[0]),
        pltpu.make_async_copy(ch_ref, ch_hbm, out_sem.at[1]),
    ]
    for c in stores:
        c.start()

    for k in range(1, n_grid):
        top_copy(k).wait_send()
    for k in range(1, n_cls):
        full_copy(k).wait()
    for n in range(nodes):
        at = n // 2 + (n % 2) * pcount
        gains_ref[n] = jnp.concatenate([full[f, at:at + 1] for f in range(f_own)], axis=0)
    stores.append(pltpu.make_async_copy(gains_ref, gains_hbm, out_sem.at[2]))
    stores[-1].start()
    for k in range(1, n_wide):
        peak_copy(k).wait_recv()
        highest = jnp.maximum(highest, peaks[k])
    best_ref[...] = highest[:, :nodes]

    for c in stores:
        c.wait()
    for k in range(1, n_wide):
        peak_copy(k).wait_send()


def store_kernel(cg, ch, gains, best, cg_out, ch_out, gains_out, best_out, *scratch):
    held, (in_sem, out_sem) = scratch[:4], scratch[4:]
    moves = []
    for src, via, dst in zip((cg, ch, gains, best), held, (cg_out, ch_out, gains_out, best_out)):
        pieces = 2 if src.shape[0] % 2 == 0 and len(src.shape) == 4 else 1
        size = src.shape[0] // pieces
        for p in range(pieces):
            moves.append([r.at[pl.ds(p * size, size)] for r in (src, via, dst)])
    first = [pltpu.make_async_copy(m[0], m[1], in_sem.at[i]) for i, m in enumerate(moves)]
    second = [pltpu.make_async_copy(m[1], m[2], out_sem.at[i]) for i, m in enumerate(moves)]
    for c in first:
        c.start()
    for a, b in zip(first, second):
        a.wait()
        b.start()
    for c in second:
        c.wait()


def per_device(bins, logits, labels, node_ids, small_flag, parent_grad, parent_hess):
    n_row = lax.axis_size("rows")
    n_cls = lax.axis_size("cls")
    n_grid = n_row * (lax.axis_size("feat") // 2)
    n_wide = 2 * n_cls
    rows_here, c_dev = logits.shape
    pcount, f_own, _, levels = parent_grad.shape
    nodes = 2 * pcount
    share = nodes // n_cls
    kc = 2 * c_dev
    lanes = levels // 2
    vmem = pl.BlockSpec(memory_space=pltpu.VMEM)
    hbm = pl.BlockSpec(memory_space=pltpu.HBM)
    dma = pltpu.SemaphoreType.DMA
    f32, bf16 = jnp.float32, jnp.bfloat16

    child_grad, child_hess, gains, best = pl.pallas_call(
        level_kernel,
        out_shape=(
            jax.ShapeDtypeStruct((nodes, f_own, c_dev, levels), f32),
            jax.ShapeDtypeStruct((nodes, f_own, c_dev, levels), f32),
            jax.ShapeDtypeStruct((nodes, f_own, levels), f32),
            jax.ShapeDtypeStruct((1, nodes), f32),
        ),
        in_specs=[hbm] * 7,
        out_specs=(hbm, hbm, hbm, vmem),
        scratch_shapes=[
            pltpu.VMEM((nodes, f_own, c_dev, levels), f32),
            pltpu.VMEM((nodes, f_own, c_dev, levels), f32),
            pltpu.VMEM((nodes, f_own, levels), f32),
            pltpu.VMEM((f_own, nodes, levels), f32),
            dma((3,)),
            pltpu.VMEM((n_row * f_own, rows_here), jnp.int32),
            pltpu.VMEM((c_dev, rows_here), f32),
            pltpu.VMEM((1, rows_here), jnp.int32),
            pltpu.VMEM((rows_here // 128, 128), jnp.int32),
            pltpu.SMEM((pcount,), jnp.int32),
            pltpu.VMEM(parent_grad.shape, f32),
            pltpu.VMEM(parent_hess.shape, f32),
            dma((7,)),
            pltpu.VMEM((n_row, f_own, rows_here + rows_here // f_own), bf16),
            pltpu.VMEM((n_row, f_own, rows_here + rows_here // f_own), bf16),
            pltpu.VMEM((f_own, rows_here, levels), bf16),
            pltpu.VMEM((n_row, kc, rows_here), bf16),
            pltpu.VMEM((n_cls, 2, rows_here), f32),
            pltpu.VMEM((f_own, pcount * kc, levels), f32),
            pltpu.VMEM((f_own, nodes, levels), f32),
            pltpu.VMEM((n_cls, nodes, levels), f32),
            pltpu.VMEM((n_grid, 1, lanes), f32),
            pltpu.VMEM((n_wide, 1, lanes), f32),
            dma((n_row,)), dma((n_row,)),
            dma((n_cls,)), dma((n_cls,)), dma((n_row,)), dma((n_row,)),
            dma((n_cls,)), dma((n_cls,)), dma((n_cls,)), dma((n_cls,)),
            dma((n_grid,)), dma((n_grid,)), dma((n_wide,)), dma((n_wide,)),
        ],
        compiler_params=pltpu.CompilerParams(
            collective_id=0, has_side_effects=True, vmem_limit_bytes=60 << 20),
        name="level_step",
    )(
        bins.T, logits.T, labels.reshape(1, rows_here), node_ids.reshape(rows_here // 128, 128),
        small_flag, parent_grad, parent_hess,
    )
    results = (child_grad, child_hess, gains, best)
    child_grad, child_hess, gains, best = pl.pallas_call(
        store_kernel,
        out_shape=tuple(jax.ShapeDtypeStruct(r.shape, r.dtype) for r in results),
        in_specs=[hbm] * 4,
        out_specs=(hbm,) * 4,
        scratch_shapes=[pltpu.VMEM(r.shape, r.dtype) for r in results] + [dma((10,)), dma((10,))],
        compiler_params=pltpu.CompilerParams(vmem_limit_bytes=60 << 20),
        name="store_results",
    )(*results)
    return child_grad, child_hess, gains, best.reshape(nodes)


def solution(mesh):
    in_specs = (
        P("rows", "feat"),
        P("rows", "cls"),
        P("rows"),
        P("rows"),
        P(),
        P(None, ("feat", "rows"), "cls", None),
        P(None, ("feat", "rows"), "cls", None),
    )
    out_specs = (
        P(None, ("feat", "rows"), "cls", None),
        P(None, ("feat", "rows"), "cls", None),
        P(None, ("feat", "rows"), None),
        P(),
    )
    return jax.shard_map(
        per_device, mesh=mesh, in_specs=in_specs, out_specs=out_specs, check_vma=False
    )
```
